512 devices in a mesh: req: 64 (over z, y), head: 8 (over x, core).
Axes of the slice: x: 4, y: 4, z: 16, core: 2. Of those that a mesh axis runs over, the one named last changes fastest.
Arguments:
- inner_input: bfloat16 [16384, 16384], P('req', 'head'), may hold values from -6 to 6
- projection_input: bfloat16 [16384, 8, 2, 128], P('req', 'head'), may hold values from -6 to 6
- step_before_bias: bfloat16 [16384, 256], P('req', 'head'), may hold values from -2 to 11
- inner_conv_taps: float32 [4, 16384], P(None, 'head'), may hold values from -3 to 3
- projection_conv_taps: float32 [4, 8, 2, 128], P(None, 'head'), may hold values from -3 to 3
- step_bias: float32 [256], P('head'), may hold values from -4.5 to -3.5
- head_decay_rate: float32 [256], P('head'), may hold values from 0.1 to 3
- head_skip_gain: float32 [256], P('head'), may hold values from 0.5 to 1.5
- group_norm_gain: float32 [16384], P('head'), may hold values from 0.5 to 1.5
- tenant: int32 [64], P('req'), may hold values from 0 to 63
- tenant_adapter_row: int32 [64], replicated, may hold values from 0 to 63, each once
- cache_holder_index: int32 [64], P('req'), may hold values from 0 to 63, as said below
- cache_slot_index: int32 [64], P('req'), may hold values from 0 to 1
- adapter_down_panels: bfloat16 [64, 16384, 64], P('req', 'head'), may hold values from -0.046875 to 0.046875
- adapter_up_panels: bfloat16 [64, 64, 8192], P('req', None, 'head'), may hold values from -0.75 to 0.75
- cached_ssm_states: bfloat16 [128, 256, 64, 128], P('req', 'head'), may hold values from -2.5 to 2.5
- inner_conv_cache: bfloat16 [128, 3, 16384], P('req', None, 'head'), may hold values from -6 to 6
- projection_conv_cache: bfloat16 [128, 3, 8, 2, 128], P('req', None, 'head'), may hold values from -6 to 6
Outputs:
- normed_output: bfloat16 [16384, 16384], P('req', 'head')
- adapter_output_term: bfloat16 [16384, 8192], P('req', 'head')
- updated_state: bfloat16 [64, 256, 64, 128], P('req', 'head')
The draws below stay inside these ranges and needn't reach their ends.
Inputs may be any that keep to these rules, and one draw needn't show every extreme that they name: `tenant_adapter_row`: every row of the adapter tables belongs to exactly one tenant. `cache_holder_index`: no two requests share a cache slot, and each index of req holds the cached states of exactly 1 request.
All inputs are finite; a program needn't handle non-finite values.
Results may differ from the reference program's by a relative error of at most 0.013.
Values may be sent and summed in bfloat16 or wider, within the bound.
No kernel may reach another device: no remote copies, remote signals or barrier semaphores. Data moves between devices by JAX's collectives and lax.ppermute only.
A program may use at most 64 MiB of HBM per device.

```python
import math
import jax
import jax.numpy as jnp
import numpy as np
from jax import lax

MODEL_WIDTH = 8192
HEADS = 256
P_SIZE = 64
N = 128
G = 8
K = 4
ADAPTER_RANK = 64
FRESH_ITEMS = 256
REQ_DEV = 1
INNER_CHANNELS = 16384
REQUESTS = 64
SUMMED_ITEMS = 16384
SLOTS_DEV = 2
SLOTS = 128
TENANT_COUNT = 64


def memo_location(key):
    base_key = jax.random.fold_in(key, 11)
    placing = jax.random.permutation(jax.random.fold_in(base_key, 1), REQUESTS)
    spread_factor = SLOTS_DEV // REQ_DEV
    side = jax.random.randint(jax.random.fold_in(base_key, 2), (REQUESTS,), 0, spread_factor)
    owner = (placing // REQ_DEV).astype(jnp.int32)
    slot = (placing % REQ_DEV * spread_factor + side).astype(jnp.int32)
    return (owner, slot)


def draw_cache_holder_index(key, part):
    return memo_location(key)[0]


def draw_cache_slot_index(key, part):
    return memo_location(key)[1]


def draw_step_before_bias(key, part):
    noise_key = jax.random.fold_in(key, 3)
    spike_seed_handle = jax.random.fold_in(key, 4)
    growth_prng_stream = jax.random.fold_in(key, 5)
    baseline_noise_part = jnp.clip(0.5 * jax.random.normal(noise_key, (SUMMED_ITEMS, HEADS), jnp.float32), -2.0, 2.0)
    spike_magnitudes = jax.random.randint(spike_seed_handle, (SUMMED_ITEMS, 1), 0, max(FRESH_ITEMS // 3, 2)) == 0
    raise_offset = jax.random.uniform(growth_prng_stream, (SUMMED_ITEMS, 1), jnp.float32, 7.0, 9.0)
    return jnp.where(spike_magnitudes, baseline_noise_part + raise_offset, baseline_noise_part).astype(jnp.bfloat16)


def draw_head_decay_rate(key, part):
    rate_key = jax.random.fold_in(key, 6)
    upper = 3.0
    dispersion_factor = jax.random.uniform(rate_key, (HEADS,), jnp.float32, math.log(0.1), math.log(upper))
    return jnp.exp(dispersion_factor).astype(jnp.float32)


def touch_ends(result, rng, low, largest):
    shape = result.shape
    place = [jax.random.randint(jax.random.fold_in(rng, axis), (), 0, shape[axis]) for axis in range(len(shape))]
    result = result.at[tuple(place)].set(low)
    longest = shape.index(max(shape))
    place[longest] = (place[longest] + 1) % shape[longest]
    return result.at[tuple(place)].set(largest)


def steps_of(key, extent, shards, smallest, top_value):
    loudness = 1.0
    for position, parts in shards:
        steps = jax.random.uniform(jax.random.fold_in(jax.random.fold_in(key, 6), position), (parts,), jnp.float32, smallest / len(shards), top_value / len(shards))
        loudness = loudness * jnp.repeat(jnp.exp(steps), extent[position] // parts).reshape((-1,) + (1,) * (len(extent) - 1 - position))
    return loudness


def rank_bounds(number_of, slope):
    weights = [(1 << 20) // math.isqrt(standing ** slope) + 1 for standing in range(1, number_of + 1)]
    width = 1 + sum(weights) // (1 << 30)
    return np.cumsum(np.array([max(1, weight // width) for weight in weights]))


def ranked(stream_key, extent, count, lean):
    table = rank_bounds(count, lean)
    pick = jax.random.randint(jax.random.fold_in(stream_key, 1), extent, 0, int(table[count - 1]))
    standing = jnp.searchsorted(jnp.asarray(table, jnp.int32), pick, side="right")
    return jax.random.permutation(jax.random.fold_in(stream_key, 2), count)[standing].astype(jnp.int32)


def centred(rng, extent, width, bound, pieces=(), kind=jnp.bfloat16):
    values = jax.random.normal(rng, extent, jnp.float32) * width
    if len(pieces) > 0:
        values = steps_of(rng, extent, pieces, -0.22, 0.18) * values
    return jnp.clip(values, min=-bound, max=bound).astype(kind)


def setup_inputs(seed: int = 0) -> dict:
    seeds = jax.random.split(jax.random.key(seed), 19)
    inner_input = centred(seeds[0], (SUMMED_ITEMS, INNER_CHANNELS), 1.0, 6.0, ((0, 64), (1, 8)))
    projection_input = centred(seeds[1], (SUMMED_ITEMS, G, 2, N), 1.0, 6.0, ((0, 64), (1, 8)))
    step_before_bias = draw_step_before_bias(jax.random.fold_in(seeds[18], 71), 0)
    inner_conv_taps = centred(seeds[3], (K, INNER_CHANNELS), K ** -0.5, 3.0, ((1, 8),), jnp.float32)
    projection_conv_taps = centred(seeds[4], (K, G, 2, N), K ** -0.5, 3.0, ((1, 8),), jnp.float32)
    step_bias = jnp.clip(-4.5 + 1.0 * jax.random.uniform(seeds[5], (HEADS,), jnp.float32) ** steps_of(seeds[5], (HEADS,), ((0, 8),), -0.2, 0.2), -4.5, -3.5)
    head_decay_rate = draw_head_decay_rate(jax.random.fold_in(seeds[18], 71), 0)
    head_skip_gain = jnp.clip(0.5 + 1.0 * jax.random.uniform(seeds[7], (HEADS,), jnp.float32) ** steps_of(seeds[7], (HEADS,), ((0, 8),), -0.2, 0.2), 0.5, 1.5)
    group_norm_gain = jnp.clip(1.0 + 0.1 * jax.random.normal(seeds[8], (INNER_CHANNELS,), jnp.float32), 0.5, 1.5)
    tenant = touch_ends(ranked(seeds[9], (REQUESTS,), TENANT_COUNT, 2), jax.random.fold_in(seeds[9], 3), 0, TENANT_COUNT - 1).astype(jnp.int32)
    tenant_adapter_row = jax.random.permutation(seeds[10], TENANT_COUNT).astype(jnp.int32)
    cache_holder_index = draw_cache_holder_index(jax.random.fold_in(seeds[18], 71), 0)
    cache_slot_index = draw_cache_slot_index(jax.random.fold_in(seeds[18], 71), 0)
    adapter_down_panels = centred(seeds[13], (TENANT_COUNT, INNER_CHANNELS, ADAPTER_RANK), INNER_CHANNELS ** -0.5, 0.046875, ((0, 64), (1, 8)))
    adapter_up_panels = centred(seeds[14], (TENANT_COUNT, ADAPTER_RANK, MODEL_WIDTH), ADAPTER_RANK ** -0.5, 0.75, ((0, 64), (2, 8)))
    cached_ssm_states = centred(seeds[15], (SLOTS, HEADS, P_SIZE, N), 0.3, 2.5, ((0, 64), (1, 8)))
    inner_conv_cache = centred(seeds[16], (SLOTS, K - 1, INNER_CHANNELS), 1.0, 6.0, ((0, 64), (2, 8)))
    projection_conv_cache = centred(seeds[17], (SLOTS, K - 1, G, 2, N), 1.0, 6.0, ((0, 64), (2, 8)))
    return {"inner_input": inner_input, "projection_input": projection_input, "step_before_bias": step_before_bias, "inner_conv_taps": inner_conv_taps, "projection_conv_taps": projection_conv_taps, "step_bias": step_bias, "head_decay_rate": head_decay_rate, "head_skip_gain": head_skip_gain, "group_norm_gain": group_norm_gain, "tenant": tenant, "tenant_adapter_row": tenant_adapter_row, "cache_holder_index": cache_holder_index, "cache_slot_index": cache_slot_index, "adapter_down_panels": adapter_down_panels, "adapter_up_panels": adapter_up_panels, "cached_ssm_states": cached_ssm_states, "inner_conv_cache": inner_conv_cache, "projection_conv_cache": projection_conv_cache}


ADAPTER_SCALE = 2.0
NORM_EPSILON = 1e-05

def causal_conv(cached, current, weight):
    joined = jnp.concatenate([cached, current], axis=0).astype(jnp.float32)
    length_value = current.shape[0]
    summed = weight[0] * joined[0:length_value]
    for tap in range(1, weight.shape[0]):
        summed = summed + weight[tap] * joined[tap:tap + length_value]
    return jax.nn.silu(summed).astype(jnp.bfloat16)

def reference(inner_input, projection_input, step_before_bias, inner_conv_taps, projection_conv_taps, step_bias, head_decay_rate, head_skip_gain, group_norm_gain, tenant, tenant_adapter_row, cache_holder_index, cache_slot_index, adapter_down_panels, adapter_up_panels, cached_ssm_states, inner_conv_cache, projection_conv_cache):
    cache_rows = (cache_holder_index * SLOTS_DEV + cache_slot_index).astype(jnp.int32)
    adapter_rows = jnp.take(tenant_adapter_row, tenant).astype(jnp.int32)
    x_blocks = inner_input.reshape(REQUESTS, FRESH_ITEMS, INNER_CHANNELS)
    bc_blocks = projection_input.reshape(REQUESTS, FRESH_ITEMS, G, 2, N)
    unprocessed_sequence_blocks = step_before_bias.reshape(REQUESTS, FRESH_ITEMS, HEADS)
    per_group = HEADS // G
    positions = jnp.arange(FRESH_ITEMS, dtype=jnp.int32)
    causal = positions[:, None] >= positions[None, :]

    def one_request(request_items):
        x_req, bc_req, raw_req, cache_row, adapter_position = request_items
        cached_state = lax.dynamic_index_in_dim(cached_ssm_states, cache_row, 0, keepdims=False)
        cached_x = lax.dynamic_index_in_dim(inner_conv_cache, cache_row, 0, keepdims=False)
        cached_bc = lax.dynamic_index_in_dim(projection_conv_cache, cache_row, 0, keepdims=False)
        down_panel = lax.dynamic_index_in_dim(adapter_down_panels, adapter_position, 0, keepdims=False)
        up_panel = lax.dynamic_index_in_dim(adapter_up_panels, adapter_position, 0, keepdims=False)
        conv_x = causal_conv(cached_x, x_req, inner_conv_taps)
        conv_bc = causal_conv(cached_bc, bc_req, projection_conv_taps)
        b_proj = conv_bc[:, :, 0, :].astype(jnp.float32)
        c_proj = conv_bc[:, :, 1, :].astype(jnp.float32)
        step_size = jax.nn.softplus(raw_req.astype(jnp.float32) + step_bias)
        log_decay = jnp.cumsum(-head_decay_rate * step_size, axis=0)
        score_bc = jnp.einsum('tgn,sgn->gts', c_proj, b_proj)
        score_heads = jnp.repeat(score_bc, per_group, axis=0)
        log_gap = log_decay.T[:, :, None] - log_decay.T[:, None, :]
        decay_factor = jnp.exp(jnp.where(causal[None], log_gap, -jnp.inf))
        mix_weights = (score_heads * decay_factor * step_size.T[:, None, :]).astype(jnp.bfloat16)
        conv_heads = conv_x.reshape(FRESH_ITEMS, HEADS, P_SIZE).astype(jnp.float32)
        intra = jnp.einsum('hts,shp->thp', mix_weights.astype(jnp.float32), conv_heads)
        c_heads = jnp.repeat(c_proj, per_group, axis=1)
        inter = jnp.einsum('thn,hpn->thp', c_heads, cached_state.astype(jnp.float32)) * jnp.exp(log_decay)[:, :, None]
        mixed = intra + inter + head_skip_gain[None, :, None] * conv_heads
        grouped = mixed.reshape(FRESH_ITEMS, G, per_group * P_SIZE)
        mean_square = lax.optimization_barrier(jnp.mean(grouped * grouped, axis=2, keepdims=True))
        normed_output = ((grouped * lax.rsqrt(mean_square + NORM_EPSILON)).reshape(FRESH_ITEMS, INNER_CHANNELS) * group_norm_gain).astype(jnp.bfloat16)
        reduced_rank = jnp.dot(normed_output, down_panel, preferred_element_type=jnp.float32).astype(jnp.bfloat16)
        adapter_output_term = (jnp.dot(reduced_rank, up_panel, preferred_element_type=jnp.float32) * ADAPTER_SCALE).astype(jnp.bfloat16)
        log_total = log_decay[-1]
        carry_weight = jnp.exp(log_total[None, :] - log_decay) * step_size
        carried = (conv_heads * carry_weight[:, :, None]).astype(jnp.bfloat16)
        b_heads = jnp.repeat(b_proj, per_group, axis=1)
        fresh_state = jnp.einsum('shp,shn->hpn', carried.astype(jnp.float32), b_heads)
        updated_state = fresh_state + jnp.exp(log_total)[:, None, None] * cached_state.astype(jnp.float32)
        return (normed_output, adapter_output_term, updated_state.astype(jnp.bfloat16))
    result_list = lax.map(one_request, (x_blocks, bc_blocks, unprocessed_sequence_blocks, cache_rows, adapter_rows))
    output_gathered, adapter_term_all, state_gathered = result_list
    return (output_gathered.reshape(SUMMED_ITEMS, INNER_CHANNELS), adapter_term_all.reshape(SUMMED_ITEMS, MODEL_WIDTH), state_gathered)
```

```python
import functools

import jax
import jax.numpy as jnp
from jax import lax
from jax.experimental import pallas as pl
from jax.experimental.pallas import tpu as pltpu
from jax.sharding import PartitionSpec as P

ADAPTER_SCALE = 2.0
NORM_EPSILON = 1e-05
F32, BF16 = jnp.float32, jnp.bfloat16
VMEM_LIMIT = 48 * 1024 * 1024


def params():
    return pltpu.CompilerParams(vmem_limit_bytes=VMEM_LIMIT)


def cost(flops, nbytes):
    return pl.CostEstimate(flops=flops, bytes_accessed=nbytes, transcendentals=0)


def smem():
    return pl.BlockSpec(memory_space=pltpu.SMEM)


def vmem():
    return pl.BlockSpec(memory_space=pltpu.VMEM)


def pack_first(tenant, table, owner, slot, down, up, convx, convbc, out):
    out[:, 0:16, :] = jnp.concatenate([down[0, 0:1024, :], down[0, 1024:2048, :]], axis=1).reshape(64, 16, 128)
    for col in range(8):
        for row in range(8):
            out[col * 8 + row, 16:24, :] = up[0, row * 8 : row * 8 + 8, col * 128 : col * 128 + 128]
    lines = lax.broadcasted_iota(jnp.int32, (8, 128), 0)
    adapter = table[tenant[0]].astype(F32)
    base = jnp.where(lines == 2, adapter, jnp.where(lines == 3, owner[0].astype(F32), slot[0].astype(F32)))
    for chunk in range(64):
        tile = base
        if chunk < 54:
            for which in range(2):
                if chunk < 48:
                    k, col = chunk // 16, chunk % 16
                    line = convx[which, k : k + 1, col * 128 : col * 128 + 128]
                else:
                    k, side = (chunk - 48) // 2, (chunk - 48) % 2
                    line = convbc[which, k, 0, side : side + 1, :]
                tile = jnp.where(lines == which, jnp.broadcast_to(line.astype(F32), (8, 128)), tile)
        out[chunk, 24:32, :] = tile.astype(BF16)


def pack_second(codes, first, states, out):
    out[:, 0:32, :] = states[0]
    lines = lax.broadcasted_iota(jnp.int32, (8, 128), 0)

    def body(j, carry):
        adapter, owner, slot = codes[0, j], codes[1, j], codes[2, j]
        out[j, 32:56, :] = first[adapter, 0:24, :]
        tile = first[owner, 24:32, :].astype(F32)
        picked = jnp.sum(jnp.where(lines == slot, tile, 0.0), axis=0, keepdims=True)
        out[j, 56:64, :] = jnp.broadcast_to(picked, (8, 128)).astype(BF16)
        return carry

    lax.fori_loop(0, 64, body, 0, unroll=8)


def pack_third(codes, second, out):
    def body(j, carry):
        out[j] = second[codes[1, j]]
        return carry

    lax.fori_loop(0, 64, body, 0, unroll=8)


def steps_kernel(raw, bias, rate, decay, decay_t, step, step_t):
    v = raw[...].astype(F32) + bias[...]
    size = jnp.maximum(v, 0.0) + jnp.log(1.0 + jnp.exp(-jnp.abs(v)))
    size = jnp.concatenate([size, jnp.zeros((256, 96), F32)], axis=1)
    drop = -rate[...] * size
    rows = lax.broadcasted_iota(jnp.int32, (256, 256), 0)
    cols = lax.broadcasted_iota(jnp.int32, (256, 256), 1)
    lower = (rows >= cols).astype(F32).astype(BF16)
    high = drop.astype(BF16)
    rest = drop - high.astype(F32)
    middle = rest.astype(BF16)
    low = (rest - middle.astype(F32)).astype(BF16)
    total = jnp.dot(lower, low, preferred_element_type=F32)
    total = total + jnp.dot(lower, middle, preferred_element_type=F32)
    total = total + jnp.dot(lower, high, preferred_element_type=F32)
    decay[...] = total
    step[...] = size
    decay_t[...] = total.T[0:32, :]
    step_t[...] = size.T[0:32, :]


def widen_kernel(decay, step, gate, carry):
    block = pl.program_id(0)
    total = decay[...]
    grow = jnp.exp(total)
    keep = jnp.exp(total[255:256, :] - total) * step[...]
    shift = lax.rem(128 - 4 * block, 128)
    grow, keep = pltpu.roll(grow, shift, 1), pltpu.roll(keep, shift, 1)
    left = lax.broadcasted_iota(jnp.int32, (256, 128), 1) < 64
    for pair in range(2):
        lo, hi = 2 * pair, 2 * pair + 1
        at = slice(pair * 128, pair * 128 + 128)
        gate[:, at] = jnp.where(left, grow[:, lo : lo + 1], grow[:, hi : hi + 1])
        carry[:, at] = jnp.where(left, keep[:, lo : lo + 1], keep[:, hi : hi + 1])


def silu(v):
    return v / (1.0 + jnp.exp(-v))


def history(convs, index):
    lines = lax.broadcasted_iota(jnp.int32, (8, 128), 0)
    old = [convs[i].astype(F32) for i in index]
    return jnp.where(lines == 5, old[0], jnp.where(lines == 6, old[1], old[2]))


def conv(pad, taps):
    out = taps[0:1, :] * pad[5:261, :]
    for k in range(1, 4):
        out = out + taps[k : k + 1, :] * pad[5 + k : 261 + k, :]
    return silu(out).astype(BF16)


def mix_kernel(
    x, bc, taps, bc_taps, convs, skip, decay, decay_t, step_t, carry,
    part, c_out, fresh, pad, pad_bc, score, b_proj,
):
    block = pl.program_id(0)

    @pl.when(block == 0)
    def _():
        for side in range(2):
            at = slice(side * 128, side * 128 + 128)
            pad_bc[0:8, at] = history(convs, [48 + side, 50 + side, 52 + side])
        pad_bc[8:264, :] = bc[...].astype(F32)
        both = conv(pad_bc, bc_taps)
        b_proj[...] = both[:, 0:128]
        c_out[...] = both[:, 128:256]
        score[...] = lax.dot_general(both[:, 128:256], both[:, 0:128], (((1,), (1,)), ((), ())), preferred_element_type=F32)

    for half in range(2):
        at = slice(half * 128, half * 128 + 128)
        col = block * 2 + half
        pad[0:8, at] = history(convs, [col, col + 16, col + 32])
    pad[8:264, :] = x[...].astype(F32)
    inner = conv(pad, taps)
    moved = pltpu.roll(decay[...], lax.rem(128 - 4 * block, 128), 1)
    rows = lax.broadcasted_iota(jnp.int32, (128, 128), 0)
    cols = lax.broadcasted_iota(jnp.int32, (128, 128), 1)
    causal = rows >= cols
    left = cols < 64
    wide = inner.astype(F32)
    for pair in range(2):
        at = slice(pair * 128, pair * 128 + 128)
        values = inner[:, at]
        top, bottom = [], []
        for side in range(2):
            head = 2 * pair + side
            here = moved[:, head : head + 1]
            there = decay_t[pl.ds(4 * block + head, 1), :]
            weight = step_t[pl.ds(4 * block + head, 1), :]
            gap = here[0:128] - there[:, 0:128]
            mix = score[0:128, 0:128] * jnp.exp(jnp.where(causal, gap, -jnp.inf)) * weight[:, 0:128]
            top.append(jnp.dot(mix.astype(BF16), values[0:128], preferred_element_type=F32))
            gap = here[128:256] - there[:, 0:128]
            mix = score[128:256, 0:128] * jnp.exp(gap) * weight[:, 0:128]
            first = mix.astype(BF16)
            gap = here[128:256] - there[:, 128:256]
            mix = score[128:256, 128:256] * jnp.exp(jnp.where(causal, gap, -jnp.inf)) * weight[:, 128:256]
            both = jnp.concatenate([first, mix.astype(BF16)], axis=1)
            bottom.append(jnp.dot(both, values, preferred_element_type=F32))
        gain = skip[:, at]
        part[0:128, at] = jnp.where(left, top[0], top[1]) + gain * wide[0:128, at]
        part[128:256, at] = jnp.where(left, bottom[0], bottom[1]) + gain * wide[128:256, at]
    carried = (wide * carry[...]).astype(BF16)
    fresh[...] = lax.dot_general(carried, b_proj[...], (((0,), (0,)), ((), ())), preferred_element_type=F32)


def state_kernel(state, c_proj, part, gate, fresh, kept, gain, down, normed, low, updated, mixed):
    c_value = c_proj[...]
    square = jnp.zeros((256, 128), F32)
    for block in range(8):
        at = slice(block * 256, block * 256 + 256)
        old = state[block * 8 : block * 8 + 8].reshape(256, 128)
        inter = lax.dot_general(c_value, old, (((1,), (1,)), ((), ())), preferred_element_type=F32)
        total = part[:, at] + inter * gate[:, at]
        mixed[:, at] = total
        square = square + total[:, 0:128] * total[:, 0:128] + total[:, 128:256] * total[:, 128:256]
        updated[0, at, :] = (fresh[at, :] + kept[at, :] * old.astype(F32)).astype(BF16)
    mean = jnp.sum(square, axis=1, keepdims=True) * (1.0 / 2048.0)
    scale = lax.rsqrt(mean + NORM_EPSILON)
    sums = []
    for side in range(2):
        acc = jnp.zeros((256, 128), F32)
        for block in range(4):
            start = side * 1024 + block * 256
            at = slice(start, start + 256)
            value = (mixed[:, at] * scale * gain[:, at]).astype(BF16)
            normed[:, at] = value
            panel = down[block * 16 : block * 16 + 16].reshape(256, 128)
            acc = acc + jnp.dot(value, panel, preferred_element_type=F32)
        sums.append(acc)
    both = sums[0] + pltpu.roll(sums[1], 64, 1)
    left = lax.broadcasted_iota(jnp.int32, (128, 128), 1) < 64
    packed = jnp.where(left, both[0:128], pltpu.roll(both[128:256], 64, 1)).astype(BF16)
    for peer in range(8):
        low[peer] = packed


def up_kernel(parts, up, out):
    total = parts[0].astype(F32)
    for peer in range(1, 8):
        total = total + parts[peer].astype(F32)
    reduced = total.astype(BF16)
    halves = [reduced[:, 0:64], reduced[:, 64:128]]
    for col in range(8):
        panel = up[col * 8 : col * 8 + 8].astype(F32).reshape(64, 128).astype(BF16)
        at = slice(col * 128, col * 128 + 128)
        for half in range(2):
            value = jnp.dot(halves[half], panel, preferred_element_type=F32) * ADAPTER_SCALE
            out[half * 128 : half * 128 + 128, at] = value.astype(BF16)


def exchange(value, axis):
    return lax.all_to_all(value, axis, split_axis=0, concat_axis=0, tiled=True)


def per_device(
    inner_input,
    projection_input,
    step_before_bias,
    inner_conv_taps,
    projection_conv_taps,
    step_bias,
    head_decay_rate,
    head_skip_gain,
    group_norm_gain,
    tenant,
    tenant_adapter_row,
    cache_holder_index,
    cache_slot_index,
    adapter_down_panels,
    adapter_up_panels,
    cached_ssm_states,
    inner_conv_cache,
    projection_conv_cache,
):
    hold = lax.optimization_barrier
    packed = jax.ShapeDtypeStruct
    sent1 = pl.pallas_call(
        pack_first,
        out_shape=packed((64, 32, 128), BF16),
        in_specs=[smem()] * 4 + [vmem()] * 4,
        out_specs=vmem(),
        compiler_params=params(),
        cost_estimate=cost(0, 2 << 20),
        name="pack_first",
    )(
        tenant, tenant_adapter_row, cache_holder_index, cache_slot_index,
        adapter_down_panels, adapter_up_panels, inner_conv_cache, projection_conv_cache,
    )
    sent1, raw = hold((sent1, step_before_bias))
    got1 = exchange(sent1, "req")
    rate = jnp.pad(head_decay_rate, (0, 96)).reshape(1, 128)
    decay, decay_t, step, step_t = pl.pallas_call(
        steps_kernel,
        out_shape=[packed((256, 128), F32), packed((32, 256), F32), packed((256, 128), F32), packed((32, 256), F32)],
        in_specs=[vmem()] * 3,
        out_specs=[vmem()] * 4,
        compiler_params=params(),
        cost_estimate=cost(6 * 256 * 256 * 128, 1 << 20),
        name="steps",
    )(raw, step_bias.reshape(1, 32), rate)
    skip_wide = jnp.repeat(head_skip_gain, 64).reshape(1, 2048)
    got1, decay, skip_wide = hold((got1, decay, skip_wide))

    me = lax.axis_index("req")
    words = got1[:, 26:29, 0].astype(jnp.int32)
    mine = jnp.sum(jnp.where(words[:, 1] == me, words[:, 2], 0))
    codes = jnp.concatenate([words.T, jnp.broadcast_to(mine, (1, 64))], axis=0)
    states = cached_ssm_states.reshape(2, 64, 32, 128)
    sent2 = pl.pallas_call(
        pack_second,
        out_shape=packed((64, 64, 128), BF16),
        grid_spec=pltpu.PrefetchScalarGridSpec(
            num_scalar_prefetch=1,
            grid=(1,),
            in_specs=[
                pl.BlockSpec((64, 32, 128), lambda i, c: (0, 0, 0)),
                pl.BlockSpec((1, 64, 32, 128), lambda i, c: (c[3, 0], 0, 0, 0)),
            ],
            out_specs=pl.BlockSpec((64, 64, 128), lambda i, c: (0, 0, 0)),
        ),
        compiler_params=params(),
        cost_estimate=cost(0, 3 << 20),
        name="pack_second",
    )(codes, got1, states)
    sent2, decay, step = hold((sent2, decay, step))
    got2 = exchange(sent2, "req")
    gate, carry = pl.pallas_call(
        widen_kernel,
        out_shape=[packed((256, 2048), F32)] * 2,
        grid=(8,),
        in_specs=[pl.BlockSpec((256, 128), lambda i: (0, 0))] * 2,
        out_specs=[pl.BlockSpec((256, 256), lambda i: (0, i))] * 2,
        compiler_params=params(),
        cost_estimate=cost(0, 6 << 20),
        name="widen",
    )(decay, step)
    kept = jnp.broadcast_to(gate[255:256, :].reshape(2048, 1), (2048, 128))
    got2, gate, carry, kept = hold((got2, gate, carry, kept))

    sent3 = pl.pallas_call(
        pack_third,
        out_shape=packed((64, 32, 128), BF16),
        grid_spec=pltpu.PrefetchScalarGridSpec(
            num_scalar_prefetch=1,
            grid=(1,),
            in_specs=[pl.BlockSpec((64, 32, 128), lambda i, c: (0, 0, 0))],
            out_specs=pl.BlockSpec((64, 32, 128), lambda i, c: (0, 0, 0)),
        ),
        compiler_params=params(),
        cost_estimate=cost(0, 1 << 20),
        name="pack_third",
    )(codes, got2)
    sent3, got2 = hold((sent3, got2))
    got3 = exchange(sent3, "req")
    part, c_proj, fresh = pl.pallas_call(
        mix_kernel,
        out_shape=[packed((256, 2048), F32), packed((256, 128), BF16), packed((2048, 128), F32)],
        grid=(8,),
        in_specs=[
            pl.BlockSpec((256, 256), lambda i: (0, i)),
            pl.BlockSpec((256, 256), lambda i: (0, 0)),
            pl.BlockSpec((4, 256), lambda i: (0, i)),
            pl.BlockSpec((4, 256), lambda i: (0, 0)),
            pl.BlockSpec((64, 8, 128), lambda i: (0, 7, 0)),
            pl.BlockSpec((1, 256), lambda i: (0, i)),
            pl.BlockSpec((256, 128), lambda i: (0, 0)),
            pl.BlockSpec((32, 256), lambda i: (0, 0)),
            pl.BlockSpec((32, 256), lambda i: (0, 0)),
            pl.BlockSpec((256, 256), lambda i: (0, i)),
        ],
        out_specs=[
            pl.BlockSpec((256, 256), lambda i: (0, i)),
            pl.BlockSpec((256, 128), lambda i: (0, 0)),
            pl.BlockSpec((256, 128), lambda i: (i, 0)),
        ],
        scratch_shapes=[
            pltpu.VMEM((264, 256), F32),
            pltpu.VMEM((264, 256), F32),
            pltpu.VMEM((256, 256), F32),
            pltpu.VMEM((256, 128), BF16),
        ],
        compiler_params=params(),
        cost_estimate=cost(2 << 30, 10 << 20),
        name="mix",
    )(
        inner_input, projection_input.reshape(256, 256), inner_conv_taps, projection_conv_taps.reshape(4, 256),
        got2, skip_wide, decay, decay_t, step_t, carry,
    )
    got3, part, c_proj, fresh = hold((got3, part, c_proj, fresh))

    normed, low, updated = pl.pallas_call(
        state_kernel,
        out_shape=[packed((256, 2048), BF16), packed((8, 128, 128), BF16), packed((1, 2048, 128), BF16)],
        grid=(1,),
        in_specs=[
            pl.BlockSpec((64, 32, 128), lambda i: (0, 0, 0)),
            pl.BlockSpec((256, 128), lambda i: (0, 0)),
            pl.BlockSpec((256, 2048), lambda i: (0, 0)),
            pl.BlockSpec((256, 2048), lambda i: (0, 0)),
            pl.BlockSpec((2048, 128), lambda i: (0, 0)),
            pl.BlockSpec((2048, 128), lambda i: (0, 0)),
            pl.BlockSpec((1, 2048), lambda i: (0, 0)),
            pl.BlockSpec((64, 16, 128), lambda i: (0, 2, 0)),
        ],
        out_specs=[
            pl.BlockSpec((256, 2048), lambda i: (0, 0)),
            pl.BlockSpec((8, 128, 128), lambda i: (0, 0, 0)),
            pl.BlockSpec((1, 2048, 128), lambda i: (0, 0, 0)),
        ],
        scratch_shapes=[pltpu.VMEM((256, 2048), F32)],
        compiler_params=params(),
        cost_estimate=cost(1 << 28, 8 << 20),
        name="state",
    )(got3, c_proj, part, gate, fresh, kept, group_norm_gain.reshape(1, 2048), got2)
    parts = exchange(low, "head")
    term = pl.pallas_call(
        up_kernel,
        out_shape=packed((256, 1024), BF16),
        grid=(1,),
        in_specs=[
            pl.BlockSpec((8, 128, 128), lambda i: (0, 0, 0)),
            pl.BlockSpec((64, 8, 128), lambda i: (0, 6, 0)),
        ],
        out_specs=pl.BlockSpec((256, 1024), lambda i: (0, 0)),
        compiler_params=params(),
        cost_estimate=cost(1 << 26, 1 << 20),
        name="up",
    )(parts, got2)
    return normed, term, updated.reshape(1, 32, 64, 128)


def solution(mesh):
    return jax.shard_map(
        per_device,
        mesh=mesh,
        in_specs=(
            P("req", "head"),
            P("req", "head", None, None),
            P("req", "head"),
            P(None, "head"),
            P(None, "head", None, None),
            P("head"),
            P("head"),
            P("head"),
            P("head"),
            P("req"),
            P(),
            P("req"),
            P("req"),
            P("req", "head", None),
            P("req", None, "head"),
            P("req", "head", None, None),
            P("req", None, "head"),
            P("req", None, "head", None, None),
        ),
        out_specs=(P("req", "head"), P("req", "head"), P("req", "head", None, None)),
        check_vma=False,
    )
```

```python
import functools

import jax
import jax.numpy as jnp
from jax import lax
from jax.experimental import pallas as pl
from jax.experimental.pallas import tpu as pltpu
from jax.sharding import PartitionSpec as P

ADAPTER_SCALE = 2.0
NORM_EPSILON = 1e-05
F32, BF16 = jnp.float32, jnp.bfloat16
MIB = 1024 * 1024


def params(mib=20):
    return pltpu.CompilerParams(vmem_limit_bytes=mib * MIB)


def cost(flops, nbytes):
    return pl.CostEstimate(flops=flops, bytes_accessed=nbytes, transcendentals=0)


def smem():
    return pl.BlockSpec(memory_space=pltpu.SMEM)


def vmem():
    return pl.BlockSpec(memory_space=pltpu.VMEM)


def pack_first(tenant, table, owner, slot, down, up, convx, convbc, states, out):
    for chunk in range(64):
        col, row = chunk // 4, chunk % 4
        out[chunk, 0:16, :] = down[row * 16 : row * 16 + 16, col * 128 : col * 128 + 128]
        col, row = chunk // 8, chunk % 8
        out[chunk, 16:24, :] = up[0, row * 8 : row * 8 + 8, col * 128 : col * 128 + 128]
    lines = lax.broadcasted_iota(jnp.int32, (8, 128), 0)
    lanes = lax.broadcasted_iota(jnp.int32, (8, 128), 1)
    adapter = table[tenant[0]].astype(F32)
    base = jnp.where(lanes == 0, adapter, jnp.where(lanes == 1, owner[0].astype(F32), slot[0].astype(F32)))
    for chunk in range(64):
        tile = base
        if chunk < 54:
            for which in range(2):
                if chunk < 48:
                    k, col = chunk // 16, chunk % 16
                    line = convx[k, which : which + 1, col * 128 : col * 128 + 128]
                else:
                    k, side = (chunk - 48) // 2, (chunk - 48) % 2
                    line = convbc[which, k, 0, side : side + 1, :]
                tile = jnp.where(lines == which, jnp.broadcast_to(line.astype(F32), (8, 128)), tile)
        tile = jnp.where(lines >= 4, pltpu.roll(states[0, chunk].astype(F32), 6, 0), tile)
        tile = jnp.where(lines >= 6, states[1, chunk].astype(F32), tile)
        out[chunk, 24:32, :] = tile.astype(BF16)


def pack_second(me, first, states, out, codes, words, sems):
    lines = lax.broadcasted_iota(jnp.int32, (8, 128), 0)
    tall = lax.broadcasted_iota(jnp.int32, (64, 8, 128), 1)
    picked = jnp.sum(jnp.where(tall == 2, first[:, 24:32, :].astype(F32), 0.0), axis=1)
    turned = jnp.concatenate([picked, jnp.zeros((64, 128), F32)], axis=0).T
    words[...] = turned[0:8, :].astype(jnp.int32)
    to_scalars = pltpu.make_async_copy(words, codes, sems.at[0])
    to_scalars.start()
    to_scalars.wait()
    mine = lax.fori_loop(0, 64, lambda j, m: jnp.where(codes[1, j] == me[0], codes[2, j], m), 0, unroll=8)
    own = pltpu.make_async_copy(states.at[mine], out.at[:, 0:32, :], sems.at[1])
    own.start()

    def panels(j, carry):
        out[j, 32:56, :] = first[codes[0, j], 0:24, :]
        return carry

    lax.fori_loop(0, 64, panels, 0, unroll=8)
    own.wait()

    def lines_of(j, carry):
        tile = first[codes[1, j], 24:32, :].astype(F32)
        line = jnp.where(codes[2, j] == 0, tile[0:1], tile[1:2])
        out[j, 24:32, :] = jnp.where(lines == 6, line, out[j, 24:32, :].astype(F32)).astype(BF16)
        return carry

    lax.fori_loop(0, 64, lines_of, 0, unroll=8)


def pack_third(codes, first, second, out):
    lines = lax.broadcasted_iota(jnp.int32, (8, 128), 0)

    def body(j, carry):
        owner = codes[1, j]
        out[j, 0:24, :] = second[owner, 0:24, :]
        rest = first[owner, 24:32, :].astype(F32)
        rest = jnp.where(codes[2, j] == 0, pltpu.roll(rest, 2, 0), rest)
        out[j, 24:32, :] = jnp.where(lines >= 6, rest, second[owner, 24:32, :].astype(F32)).astype(BF16)
        return carry

    lax.fori_loop(0, 64, body, 0, unroll=8)


def steps_kernel(raw, bias, rate, decay, decay_t, step, step_t):
    v = raw[...].astype(F32) + bias[...]
    size = jnp.maximum(v, 0.0) + jnp.log(1.0 + jnp.exp(-jnp.abs(v)))
    size = jnp.concatenate([size, jnp.zeros((256, 96), F32)], axis=1)
    drop = -rate[...] * size
    rows = lax.broadcasted_iota(jnp.int32, (256, 256), 0)
    cols = lax.broadcasted_iota(jnp.int32, (256, 256), 1)
    lower = (rows >= cols).astype(F32).astype(BF16)
    high = drop.astype(BF16)
    rest = drop - high.astype(F32)
    middle = rest.astype(BF16)
    low = (rest - middle.astype(F32)).astype(BF16)
    total = jnp.dot(lower, low, preferred_element_type=F32)
    total = total + jnp.dot(lower, middle, preferred_element_type=F32)
    total = total + jnp.dot(lower, high, preferred_element_type=F32)
    decay[...] = total
    step[...] = size
    decay_t[...] = total.T[0:32, :]
    step_t[...] = size.T[0:32, :]


def widen_kernel(decay, step, gate, carry, kept):
    block = pl.program_id(0)
    total = decay[...]
    grow = jnp.exp(total)
    keep = jnp.exp(total[255:256, :] - total) * step[...]
    shift = lax.rem(128 - 4 * block, 128)
    grow, keep = pltpu.roll(grow, shift, 1), pltpu.roll(keep, shift, 1)
    left = lax.broadcasted_iota(jnp.int32, (256, 128), 1) < 64
    for pair in range(2):
        lo, hi = 2 * pair, 2 * pair + 1
        at = slice(pair * 128, pair * 128 + 128)
        gate[:, at] = jnp.where(left, grow[:, lo : lo + 1], grow[:, hi : hi + 1])
        carry[:, at] = jnp.where(left, keep[:, lo : lo + 1], keep[:, hi : hi + 1])
    for head in range(4):
        kept[head * 64 : head * 64 + 64, :] = jnp.broadcast_to(grow[255:256, head : head + 1], (64, 128))


def silu(v):
    return v / (1.0 + jnp.exp(-v))


def history(convs, index):
    lines = lax.broadcasted_iota(jnp.int32, (8, 128), 0)
    old = [convs[i].astype(F32)[6:7, :] for i in index]
    return jnp.where(lines == 5, old[0], jnp.where(lines == 6, old[1], old[2]))


def conv(pad, taps):
    out = taps[0:1, :] * pad[5:261, :]
    for k in range(1, 4):
        out = out + taps[k : k + 1, :] * pad[5 + k : 261 + k, :]
    return silu(out).astype(BF16)


def mix_kernel(
    x, bc, taps, bc_taps, convs, skip, decay, decay_t, step_t, carry,
    part, c_out, fresh, pad, pad_bc, score, b_proj,
):
    block = pl.program_id(0)

    @pl.when(block == 0)
    def _():
        for side in range(2):
            at = slice(side * 128, side * 128 + 128)
            pad_bc[0:8, at] = history(convs, [48 + side, 50 + side, 52 + side])
        pad_bc[8:264, :] = bc[...].astype(F32)
        both = conv(pad_bc, bc_taps)
        b_proj[...] = both[:, 0:128]
        c_out[...] = both[:, 128:256]
        score[...] = lax.dot_general(both[:, 128:256], both[:, 0:128], (((1,), (1,)), ((), ())), preferred_element_type=F32)

    for half in range(2):
        at = slice(half * 128, half * 128 + 128)
        col = block * 2 + half
        pad[0:8, at] = history(convs, [col, col + 16, col + 32])
    pad[8:264, :] = x[...].astype(F32)
    inner = conv(pad, taps)
    moved = pltpu.roll(decay[...], lax.rem(128 - 4 * block, 128), 1)
    rows = lax.broadcasted_iota(jnp.int32, (128, 128), 0)
    cols = lax.broadcasted_iota(jnp.int32, (128, 128), 1)
    causal = rows >= cols
    left = cols < 64
    wide = inner.astype(F32)
    for pair in range(2):
        at = slice(pair * 128, pair * 128 + 128)
        values = inner[:, at]
        top, bottom = [], []
        for side in range(2):
            head = 2 * pair + side
            here = moved[:, head : head + 1]
            there = decay_t[pl.ds(4 * block + head, 1), :]
            weight = step_t[pl.ds(4 * block + head, 1), :]
            gap = here[0:128] - there[:, 0:128]
            mix = score[0:128, 0:128] * jnp.exp(jnp.where(causal, gap, -jnp.inf)) * weight[:, 0:128]
            top.append(jnp.dot(mix.astype(BF16), values[0:128], preferred_element_type=F32))
            gap = here[128:256] - there[:, 0:128]
            mix = score[128:256, 0:128] * jnp.exp(gap) * weight[:, 0:128]
            first = mix.astype(BF16)
            gap = here[128:256] - there[:, 128:256]
            mix = score[128:256, 128:256] * jnp.exp(jnp.where(causal, gap, -jnp.inf)) * weight[:, 128:256]
            both = jnp.concatenate([first, mix.astype(BF16)], axis=1)
            bottom.append(jnp.dot(both, values, preferred_element_type=F32))
        gain = skip[:, at]
        part[0:128, at] = jnp.where(left, top[0], top[1]) + gain * wide[0:128, at]
        part[128:256, at] = jnp.where(left, bottom[0], bottom[1]) + gain * wide[128:256, at]
    carried = (wide * carry[...]).astype(BF16)
    fresh[...] = lax.dot_general(carried, b_proj[...], (((0,), (0,)), ((), ())), preferred_element_type=F32)


def state_kernel(state, c_far, part_far, gate_far, gain, panels, normed, low, mixed, part, gate, tile, c_proj, sems):
    fetch = pltpu.make_async_copy(c_far, c_proj, sems.at[0, 8])
    fetch.start()
    copies = []
    for block in range(8):
        at = pl.ds(block * 256, 256)
        copies.append(pltpu.make_async_copy(part_far.at[:, at], part.at[:, at], sems.at[0, block]))
        copies.append(pltpu.make_async_copy(gate_far.at[:, at], gate.at[:, at], sems.at[1, block]))
    for copy in copies:
        copy.start()
    fetch.wait()
    c_value = c_proj[...]
    square = jnp.zeros((256, 128), F32)
    for block in range(8):
        at = slice(block * 256, block * 256 + 256)
        old = state[block * 8 : block * 8 + 8].reshape(256, 128)
        inter = lax.dot_general(c_value, old, (((1,), (1,)), ((), ())), preferred_element_type=F32)
        copies[2 * block].wait()
        copies[2 * block + 1].wait()
        total = part[:, at] + inter * gate[:, at]
        mixed[:, at] = total
        square = square + total[:, 0:128] * total[:, 0:128] + total[:, 128:256] * total[:, 128:256]
    mean = jnp.sum(square, axis=1, keepdims=True) * (1.0 / 2048.0)
    scale = lax.rsqrt(mean + NORM_EPSILON)
    acc = jnp.zeros((256, 64), F32)
    for col in range(16):
        at = slice(col * 128, col * 128 + 128)
        value = (mixed[:, at] * scale * gain[:, at]).astype(BF16)
        normed[:, at] = value
        panel = panels[col * 4 : col * 4 + 4, 32:48, :].reshape(64, 128)
        acc = acc + lax.dot_general(value, panel, (((1,), (1,)), ((), ())), preferred_element_type=F32)
    tile[...] = jnp.concatenate([acc[0:128], acc[128:256]], axis=1).astype(BF16)
    copies = [pltpu.make_async_copy(tile, low.at[peer], sems.at[0, peer]) for peer in range(8)]
    for copy in copies:
        copy.start()
    for copy in copies:
        copy.wait()


def update_kernel(state, fresh, kept, updated):
    updated[0] = (fresh[...] + kept[...] * state[...].reshape(2048, 128).astype(F32)).astype(BF16)


def up_kernel(parts, up, out):
    total = parts[0].astype(F32)
    for peer in range(1, 8):
        total = total + parts[peer].astype(F32)
    reduced = total.astype(BF16)
    halves = [reduced[:, 0:64], reduced[:, 64:128]]
    for col in range(8):
        panel = up[col * 8 : col * 8 + 8, 48:56, :].astype(F32).reshape(64, 128).astype(BF16)
        at = slice(col * 128, col * 128 + 128)
        for half in range(2):
            value = jnp.dot(halves[half], panel, preferred_element_type=F32) * ADAPTER_SCALE
            out[half * 128 : half * 128 + 128, at] = value.astype(BF16)


def exchange(value, axis):
    return lax.all_to_all(value, axis, split_axis=0, concat_axis=0, tiled=True)


def per_device(
    inner_input,
    projection_input,
    step_before_bias,
    inner_conv_taps,
    projection_conv_taps,
    step_bias,
    head_decay_rate,
    head_skip_gain,
    group_norm_gain,
    tenant,
    tenant_adapter_row,
    cache_holder_index,
    cache_slot_index,
    adapter_down_panels,
    adapter_up_panels,
    cached_ssm_states,
    inner_conv_cache,
    projection_conv_cache,
):
    hold = lax.optimization_barrier
    packed = jax.ShapeDtypeStruct
    whole = lambda *shape: pl.BlockSpec(shape, lambda i: (0,) * len(shape))
    far = pl.BlockSpec(memory_space=pltpu.HBM)
    states = cached_ssm_states.reshape(2, 64, 32, 128)
    sent1 = pl.pallas_call(
        pack_first,
        out_shape=packed((64, 32, 128), BF16),
        grid=(1,),
        in_specs=[smem()] * 4
        + [
            whole(64, 2048),
            whole(1, 64, 1024),
            whole(3, 2, 2048),
            whole(2, 3, 1, 2, 128),
            pl.BlockSpec((2, 64, 8, 128), lambda i: (0, 0, 3, 0)),
        ],
        out_specs=whole(64, 32, 128),
        compiler_params=params(60),
        cost_estimate=cost(0, 2 << 20),
        name="pack_first",
    )(
        tenant, tenant_adapter_row, cache_holder_index, cache_slot_index,
        jnp.swapaxes(adapter_down_panels, 1, 2).reshape(64, 2048), adapter_up_panels,
        jnp.swapaxes(inner_conv_cache, 0, 1), projection_conv_cache, states,
    )
    sent1, raw = hold((sent1, step_before_bias))
    got1 = exchange(sent1, "req")
    rate = jnp.pad(head_decay_rate, (0, 96)).reshape(1, 128)
    decay, decay_t, step, step_t = pl.pallas_call(
        steps_kernel,
        out_shape=[packed((256, 128), F32), packed((32, 256), F32), packed((256, 128), F32), packed((32, 256), F32)],
        in_specs=[vmem()] * 3,
        out_specs=[vmem()] * 4,
        compiler_params=params(),
        cost_estimate=cost(6 * 256 * 256 * 128, 1 << 20),
        name="steps",
    )(raw, step_bias.reshape(1, 32), rate)
    skip_wide = jnp.repeat(head_skip_gain, 64).reshape(1, 2048)
    me = lax.axis_index("req").astype(jnp.int32).reshape(1)
    got1, decay, skip_wide, me = hold((got1, decay, skip_wide, me))

    sent2, codes = pl.pallas_call(
        pack_second,
        out_shape=[packed((64, 56, 128), BF16), packed((8, 128), jnp.int32)],
        in_specs=[smem(), vmem(), pl.BlockSpec(memory_space=pl.ANY)],
        out_specs=[vmem(), smem()],
        scratch_shapes=[pltpu.VMEM((8, 128), jnp.int32), pltpu.SemaphoreType.DMA((2,))],
        compiler_params=params(52),
        cost_estimate=cost(0, 3 << 20),
        name="pack_second",
    )(me, got1, states)
    sent2, decay, step = hold((sent2, decay, step))
    got2 = exchange(sent2, "req")
    gate, carry, kept = pl.pallas_call(
        widen_kernel,
        out_shape=[packed((256, 2048), F32)] * 2 + [packed((2048, 128), F32)],
        grid=(8,),
        in_specs=[pl.BlockSpec((256, 128), lambda i: (0, 0))] * 2,
        out_specs=[pl.BlockSpec((256, 256), lambda i: (0, i))] * 2 + [pl.BlockSpec((256, 128), lambda i: (i, 0))],
        compiler_params=params(),
        cost_estimate=cost(0, 6 << 20),
        name="widen",
    )(decay, step)
    got2, gate, carry, kept = hold((got2, gate, carry, kept))

    sent3 = pl.pallas_call(
        pack_third,
        out_shape=packed((64, 32, 128), BF16),
        in_specs=[smem(), vmem(), vmem()],
        out_specs=vmem(),
        compiler_params=params(52),
        cost_estimate=cost(0, 1 << 20),
        name="pack_third",
    )(codes, got1, got2)
    sent3, got2 = hold((sent3, got2))
    got3 = exchange(sent3, "req")
    part, c_proj, fresh = pl.pallas_call(
        mix_kernel,
        out_shape=[packed((256, 2048), F32), packed((256, 128), BF16), packed((2048, 128), F32)],
        grid=(8,),
        in_specs=[
            pl.BlockSpec((256, 256), lambda i: (0, i)),
            pl.BlockSpec((256, 256), lambda i: (0, 0)),
            pl.BlockSpec((4, 256), lambda i: (0, i)),
            pl.BlockSpec((4, 256), lambda i: (0, 0)),
            pl.BlockSpec((64, 8, 128), lambda i: (0, 3, 0)),
            pl.BlockSpec((1, 256), lambda i: (0, i)),
            pl.BlockSpec((256, 128), lambda i: (0, 0)),
            pl.BlockSpec((32, 256), lambda i: (0, 0)),
            pl.BlockSpec((32, 256), lambda i: (0, 0)),
            pl.BlockSpec((256, 256), lambda i: (0, i)),
        ],
        out_specs=[
            pl.BlockSpec((256, 256), lambda i: (0, i)),
            pl.BlockSpec((256, 128), lambda i: (0, 0)),
            pl.BlockSpec((256, 128), lambda i: (i, 0)),
        ],
        scratch_shapes=[
            pltpu.VMEM((264, 256), F32),
            pltpu.VMEM((264, 256), F32),
            pltpu.VMEM((256, 256), F32),
            pltpu.VMEM((256, 128), BF16),
        ],
        compiler_params=params(),
        cost_estimate=cost(2 << 30, 10 << 20),
        name="mix",
    )(
        inner_input, projection_input.reshape(256, 256), inner_conv_taps, projection_conv_taps.reshape(4, 256),
        got2, skip_wide, decay, decay_t, step_t, carry,
    )
    got3, part, c_proj, fresh = hold((got3, part, c_proj, fresh))

    normed, low = pl.pallas_call(
        state_kernel,
        out_shape=[packed((256, 2048), BF16), packed((8, 128, 128), BF16)],
        grid=(1,),
        in_specs=[whole(64, 32, 128), far, far, far, whole(1, 2048), whole(64, 56, 128)],
        out_specs=[whole(256, 2048), far],
        scratch_shapes=[pltpu.VMEM((256, 2048), F32)] * 3
        + [pltpu.VMEM((128, 128), BF16), pltpu.VMEM((256, 128), BF16), pltpu.SemaphoreType.DMA((2, 9))],
        compiler_params=params(50),
        cost_estimate=cost(1 << 28, 8 << 20),
        name="state",
    )(got3, c_proj, part, gate, group_norm_gain.reshape(1, 2048), got2)
    low, fresh = hold((low, fresh))
    parts = exchange(low, "head")
    updated = pl.pallas_call(
        update_kernel,
        out_shape=packed((1, 2048, 128), BF16),
        in_specs=[vmem()] * 3,
        out_specs=vmem(),
        compiler_params=params(),
        cost_estimate=cost(1 << 20, 3 << 20),
        name="update",
    )(got3, fresh, kept)
    parts, updated = hold((parts, updated))
    term = pl.pallas_call(
        up_kernel,
        out_shape=packed((256, 1024), BF16),
        in_specs=[vmem()] * 2,
        out_specs=vmem(),
        compiler_params=params(),
        cost_estimate=cost(1 << 26, 1 << 20),
        name="up",
    )(parts, got2)
    return normed, term, updated.reshape(1, 32, 64, 128)


def solution(mesh):
    return jax.shard_map(
        per_device,
        mesh=mesh,
        in_specs=(
            P("req", "head"),
            P("req", "head", None, None),
            P("req", "head"),
            P(None, "head"),
            P(None, "head", None, None),
            P("head"),
            P("head"),
            P("head"),
            P("head"),
            P("req"),
            P(),
            P("req"),
            P("req"),
            P("req", "head", None),
            P("req", None, "head"),
            P("req", "head", None, None),
            P("req", None, "head"),
            P("req", None, "head", None, None),
        ),
        out_specs=(P("req", "head"), P("req", "head"), P("req", "head", None, None)),
        check_vma=False,
    )
```

```python
import functools

import jax
import jax.numpy as jnp
from jax import lax
from jax.experimental import pallas as pl
from jax.experimental.pallas import tpu as pltpu
from jax.sharding import PartitionSpec as P

ADAPTER_SCALE = 2.0
NORM_EPSILON = 1e-05
F32, BF16 = jnp.float32, jnp.bfloat16
MIB = 1024 * 1024


def params(mib=20):
    return pltpu.CompilerParams(vmem_limit_bytes=mib * MIB)


def cost(flops, nbytes):
    return pl.CostEstimate(flops=flops, bytes_accessed=nbytes, transcendentals=0)


def smem():
    return pl.BlockSpec(memory_space=pltpu.SMEM)


def vmem():
    return pl.BlockSpec(memory_space=pltpu.VMEM)


def pack_first(tenant, table, owner, slot, down, up, convx, convbc, states, out):
    for chunk in range(64):
        col, row = chunk // 4, chunk % 4
        out[chunk, 0:16, :] = down[row * 16 : row * 16 + 16, col * 128 : col * 128 + 128]
        col, row = chunk // 8, chunk % 8
        out[chunk, 16:24, :] = up[0, row * 8 : row * 8 + 8, col * 128 : col * 128 + 128]
    lines = lax.broadcasted_iota(jnp.int32, (8, 128), 0)
    lanes = lax.broadcasted_iota(jnp.int32, (8, 128), 1)
    adapter = table[tenant[0]].astype(F32)
    base = jnp.where(lanes == 0, adapter, jnp.where(lanes == 1, owner[0].astype(F32), slot[0].astype(F32)))
    for chunk in range(64):
        tile = base
        if chunk < 54:
            for which in range(2):
                if chunk < 48:
                    k, col = chunk // 16, chunk % 16
                    line = convx[k, which : which + 1, col * 128 : col * 128 + 128]
                else:
                    k, side = (chunk - 48) // 2, (chunk - 48) % 2
                    line = convbc[which, k, 0, side : side + 1, :]
                tile = jnp.where(lines == which, jnp.broadcast_to(line.astype(F32), (8, 128)), tile)
        tile = jnp.where(lines >= 4, pltpu.roll(states[0, chunk].astype(F32), 6, 0), tile)
        tile = jnp.where(lines >= 6, states[1, chunk].astype(F32), tile)
        out[chunk, 24:32, :] = tile.astype(BF16)


def pack_second(me, first, states, out, codes, words, sems):
    lines = lax.broadcasted_iota(jnp.int32, (8, 128), 0)
    tall = lax.broadcasted_iota(jnp.int32, (64, 8, 128), 1)
    picked = jnp.sum(jnp.where(tall == 2, first[:, 24:32, :].astype(F32), 0.0), axis=1)
    turned = jnp.concatenate([picked, jnp.zeros((64, 128), F32)], axis=0).T
    words[...] = turned[0:8, :].astype(jnp.int32)
    to_scalars = pltpu.make_async_copy(words, codes, sems.at[0])
    to_scalars.start()
    to_scalars.wait()
    mine = lax.fori_loop(0, 64, lambda j, m: jnp.where(codes[1, j] == me[0], codes[2, j], m), 0, unroll=8)
    own = pltpu.make_async_copy(states.at[mine], out.at[:, 0:32, :], sems.at[1])
    own.start()

    def panels(j, carry):
        out[j, 32:56, :] = first[codes[0, j], 0:24, :]
        return carry

    lax.fori_loop(0, 64, panels, 0, unroll=8)
    own.wait()

    def lines_of(j, carry):
        tile = first[codes[1, j], 24:32, :].astype(F32)
        line = jnp.where(codes[2, j] == 0, tile[0:1], tile[1:2])
        out[j, 24:32, :] = jnp.where(lines == 6, line, out[j, 24:32, :].astype(F32)).astype(BF16)
        return carry

    lax.fori_loop(0, 64, lines_of, 0, unroll=8)


def pack_third(codes, first, second, out):
    lines = lax.broadcasted_iota(jnp.int32, (8, 128), 0)

    def body(j, carry):
        owner = codes[1, j]
        out[j, 0:24, :] = second[owner, 0:24, :]
        rest = first[owner, 24:32, :].astype(F32)
        rest = jnp.where(codes[2, j] == 0, pltpu.roll(rest, 2, 0), rest)
        out[j, 24:32, :] = jnp.where(lines >= 6, rest, second[owner, 24:32, :].astype(F32)).astype(BF16)
        return carry

    lax.fori_loop(0, 64, body, 0, unroll=8)


def silu(v):
    return v / (1.0 + jnp.exp(-v))


def history(convs, index):
    lines = lax.broadcasted_iota(jnp.int32, (8, 128), 0)
    old = [convs[i].astype(F32)[6:7, :] for i in index]
    return jnp.where(lines == 5, old[0], jnp.where(lines == 6, old[1], old[2]))


def conv(pad, taps, count):
    out = taps[0:1, :] * pad[5 : 5 + count, :]
    for k in range(1, 4):
        out = out + taps[k : k + 1, :] * pad[5 + k : 5 + count + k, :]
    return silu(out)


def widened(value, lo, hi):
    left = lax.broadcasted_iota(jnp.int32, (value.shape[0], 128), 1) < 64
    return jnp.where(left, value[:, lo : lo + 1], value[:, hi : hi + 1])


def wide_row(row):
    return jnp.concatenate([row, jnp.zeros((1, 96), F32)], axis=1)


def dots(a, b, left, right):
    return lax.dot_general(a, b, (((left,), (right,)), ((), ())), preferred_element_type=F32)


def scan_kernel(flag, x, bc, taps, bc_taps, raw, bias, rate, skip, *rest):
    outs, (pad, pad_bc, score) = rest[-13:-3], rest[-3:]
    old = rest[:-13]
    part, gate, fresh, kept, c_out, b_out, decay, decay_t, step, step_t = outs
    block = pl.program_id(0)
    active = flag[0] == 1

    if old:

        @pl.when(jnp.logical_and(jnp.logical_not(active), block == 0))
        def _():
            for source, target in zip(old, outs):
                target[...] = source[...]

    @pl.when(jnp.logical_and(active, block == 0))
    def _():
        v = jnp.concatenate([raw[...].astype(F32), jnp.zeros((96, 256), F32)], axis=0).T + wide_row(bias[...])
        size = jnp.maximum(v, 0.0) + jnp.log(1.0 + jnp.exp(-jnp.abs(v)))
        drop = -wide_row(rate[...]) * size
        rows = lax.broadcasted_iota(jnp.int32, (256, 256), 0)
        cols = lax.broadcasted_iota(jnp.int32, (256, 256), 1)
        lower = (rows >= cols).astype(F32).astype(BF16)
        high = drop.astype(BF16)
        spare = drop - high.astype(F32)
        middle = spare.astype(BF16)
        low = (spare - middle.astype(F32)).astype(BF16)
        total = jnp.dot(lower, low, preferred_element_type=F32)
        total = total + jnp.dot(lower, middle, preferred_element_type=F32)
        total = total + jnp.dot(lower, high, preferred_element_type=F32)
        decay[...] = total
        step[...] = size
        decay_t[...] = total.T[0:32, :]
        step_t[...] = size.T[0:32, :]
        pad_bc[0:8, :] = jnp.zeros((8, 256), F32)
        pad_bc[8:264, :] = bc[...].astype(F32)
        both = jnp.where(rows >= 3, conv(pad_bc, bc_taps, 256), 0.0).astype(BF16)
        b_out[...] = both[:, 0:128]
        c_out[...] = both[:, 128:256]
        score[...] = dots(both[:, 128:256], both[:, 0:128], 1, 1)

    @pl.when(active)
    def _():
        pad[0:8, :] = jnp.zeros((8, 256), F32)
        pad[8:264, :] = x[...].astype(F32)
        tall = lax.broadcasted_iota(jnp.int32, (256, 256), 0)
        inner = jnp.where(tall >= 3, conv(pad, taps, 256), 0.0).astype(BF16)
        total = decay[...]
        shift = lax.rem(128 - 4 * block, 128)
        moved = pltpu.roll(total, shift, 1)
        grow = jnp.exp(moved)
        keep = pltpu.roll(jnp.exp(total[255:256, :] - total) * step[...], shift, 1)
        gains = pltpu.roll(jnp.broadcast_to(wide_row(skip[...]), (8, 128)), shift, 1)
        rows = lax.broadcasted_iota(jnp.int32, (128, 128), 0)
        cols = lax.broadcasted_iota(jnp.int32, (128, 128), 1)
        causal = rows >= cols
        left = cols < 64
        wide = inner.astype(F32)
        for pair in range(2):
            lo, hi = 2 * pair, 2 * pair + 1
            at = slice(pair * 128, pair * 128 + 128)
            values = inner[:, at]
            top, bottom = [], []
            for head in (lo, hi):
                here = moved[:, head : head + 1]
                there = decay_t[pl.ds(4 * block + head, 1), :]
                weight = step_t[pl.ds(4 * block + head, 1), :]
                gap = here[0:128] - there[:, 0:128]
                mix = score[0:128, 0:128] * jnp.exp(jnp.where(causal, gap, -jnp.inf)) * weight[:, 0:128]
                top.append(jnp.dot(mix.astype(BF16), values[0:128], preferred_element_type=F32))
                gap = here[128:256] - there[:, 0:128]
                mix = score[128:256, 0:128] * jnp.exp(gap) * weight[:, 0:128]
                early = mix.astype(BF16)
                gap = here[128:256] - there[:, 128:256]
                mix = score[128:256, 128:256] * jnp.exp(jnp.where(causal, gap, -jnp.inf)) * weight[:, 128:256]
                both = jnp.concatenate([early, mix.astype(BF16)], axis=1)
                bottom.append(jnp.dot(both, values, preferred_element_type=F32))
            gain = widened(gains[0:1, :], lo, hi)
            part[0:128, at] = jnp.where(left, top[0], top[1]) + gain * wide[0:128, at]
            part[128:256, at] = jnp.where(left, bottom[0], bottom[1]) + gain * wide[128:256, at]
            gate[:, at] = widened(grow, lo, hi)
            carried = (wide[:, at] * widened(keep, lo, hi)).astype(BF16)
            fresh[at, :] = dots(carried, b_out[...], 0, 0)
        for head in range(4):
            kept[head * 64 : head * 64 + 64, :] = jnp.broadcast_to(grow[255:256, head : head + 1], (64, 128))


def early_rows(
    x, bc, taps, bc_taps, convs, skip, c_main, decay, decay_t, step, step_t, part_in, fresh_in,
    part, fresh, c_out, pad, pad_bc, score, b_proj,
):
    block = pl.program_id(0)
    short = lax.broadcasted_iota(jnp.int32, (8, 256), 0) < 3
    rest = jnp.zeros((120, 128), F32)

    @pl.when(block == 0)
    def _():
        for side in range(2):
            at = slice(side * 128, side * 128 + 128)
            pad_bc[0:8, at] = history(convs, [48 + side, 50 + side, 52 + side])
        pad_bc[8:16, :] = bc[0:8, :].astype(F32)
        both = jnp.where(short, conv(pad_bc, bc_taps, 8), 0.0)
        b_proj[...] = jnp.concatenate([both[:, 0:128], rest], axis=0).astype(BF16)
        c_all = c_main[...].astype(F32)
        c_all = jnp.concatenate([c_all[0:8] + both[:, 128:256], c_all[8:256]], axis=0).astype(BF16)
        c_out[...] = c_all
        score[...] = dots(c_all, b_proj[...], 1, 1)

    for half in range(2):
        at = slice(half * 128, half * 128 + 128)
        col = block * 2 + half
        pad[0:8, at] = history(convs, [col, col + 16, col + 32])
    pad[8:16, :] = x[0:8, :].astype(F32)
    inner = jnp.where(short, conv(pad, taps, 8), 0.0).astype(BF16).astype(F32)
    total = decay[...]
    shift = lax.rem(128 - 4 * block, 128)
    moved = pltpu.roll(total, shift, 1)
    keep = pltpu.roll(jnp.exp(total[255:256, :] - total[0:8, :]) * step[0:8, :], shift, 1)
    gains = pltpu.roll(jnp.broadcast_to(wide_row(skip[...]), (8, 128)), shift, 1)
    rows = lax.broadcasted_iota(jnp.int32, (256, 128), 0)
    cols = lax.broadcasted_iota(jnp.int32, (256, 128), 1)
    causal = rows >= cols
    left = cols < 64
    for pair in range(2):
        lo, hi = 2 * pair, 2 * pair + 1
        at = slice(pair * 128, pair * 128 + 128)
        values = jnp.concatenate([inner[:, at], rest], axis=0).astype(BF16)
        added = []
        for head in (lo, hi):
            gap = moved[:, head : head + 1] - decay_t[pl.ds(4 * block + head, 1), :][:, 0:128]
            weight = step_t[pl.ds(4 * block + head, 1), :][:, 0:128]
            mix = score[...] * jnp.exp(jnp.where(causal, gap, -jnp.inf)) * weight
            added.append(jnp.dot(mix.astype(BF16), values, preferred_element_type=F32))
        part[:, at] = part_in[:, at] + jnp.where(left, added[0], added[1])
        part[0:8, at] = part[0:8, at] + widened(gains[0:1, :], lo, hi) * inner[:, at]
        carried = (inner[:, at] * widened(keep, lo, hi)).astype(BF16).astype(F32)
        carried = jnp.concatenate([carried, rest], axis=0).astype(BF16)
        fresh[at, :] = fresh_in[at, :] + dots(carried, b_proj[...], 0, 0)


def state_kernel(state, c_far, part_far, gate_far, gain, panels, normed, low, mixed, part, gate, tile, c_proj, sems):
    fetch = pltpu.make_async_copy(c_far, c_proj, sems.at[0, 8])
    fetch.start()
    copies = []
    for block in range(8):
        at = pl.ds(block * 256, 256)
        copies.append(pltpu.make_async_copy(part_far.at[:, at], part.at[:, at], sems.at[0, block]))
        copies.append(pltpu.make_async_copy(gate_far.at[:, at], gate.at[:, at], sems.at[1, block]))
    for copy in copies:
        copy.start()
    fetch.wait()
    c_value = c_proj[...]
    square = jnp.zeros((256, 128), F32)
    for block in range(8):
        at = slice(block * 256, block * 256 + 256)
        old = state[block * 8 : block * 8 + 8].reshape(256, 128)
        inter = lax.dot_general(c_value, old, (((1,), (1,)), ((), ())), preferred_element_type=F32)
        copies[2 * block].wait()
        copies[2 * block + 1].wait()
        total = part[:, at] + inter * gate[:, at]
        mixed[:, at] = total
        square = square + total[:, 0:128] * total[:, 0:128] + total[:, 128:256] * total[:, 128:256]
    mean = jnp.sum(square, axis=1, keepdims=True) * (1.0 / 2048.0)
    scale = lax.rsqrt(mean + NORM_EPSILON)
    acc = jnp.zeros((256, 64), F32)
    for col in range(16):
        at = slice(col * 128, col * 128 + 128)
        value = (mixed[:, at] * scale * gain[:, at]).astype(BF16)
        normed[:, at] = value
        panel = panels[col * 4 : col * 4 + 4, 32:48, :].reshape(64, 128)
        acc = acc + lax.dot_general(value, panel, (((1,), (1,)), ((), ())), preferred_element_type=F32)
    tile[...] = jnp.concatenate([acc[0:128], acc[128:256]], axis=1).astype(BF16)
    copies = [pltpu.make_async_copy(tile, low.at[peer], sems.at[0, peer]) for peer in range(8)]
    for copy in copies:
        copy.start()
    for copy in copies:
        copy.wait()


def update_kernel(state, fresh, kept, updated):
    updated[0] = (fresh[...] + kept[...] * state[...].reshape(2048, 128).astype(F32)).astype(BF16)


def up_kernel(parts, up, out):
    total = parts[0].astype(F32)
    for peer in range(1, 8):
        total = total + parts[peer].astype(F32)
    reduced = total.astype(BF16)
    halves = [reduced[:, 0:64], reduced[:, 64:128]]
    for col in range(8):
        panel = up[col * 8 : col * 8 + 8, 48:56, :].astype(F32).reshape(64, 128).astype(BF16)
        at = slice(col * 128, col * 128 + 128)
        for half in range(2):
            value = jnp.dot(halves[half], panel, preferred_element_type=F32) * ADAPTER_SCALE
            out[half * 128 : half * 128 + 128, at] = value.astype(BF16)


def exchange(value, axis):
    return lax.all_to_all(value, axis, split_axis=0, concat_axis=0, tiled=True)


def per_device(
    inner_input,
    projection_input,
    step_before_bias,
    inner_conv_taps,
    projection_conv_taps,
    step_bias,
    head_decay_rate,
    head_skip_gain,
    group_norm_gain,
    tenant,
    tenant_adapter_row,
    cache_holder_index,
    cache_slot_index,
    adapter_down_panels,
    adapter_up_panels,
    cached_ssm_states,
    inner_conv_cache,
    projection_conv_cache,
):
    hold = lax.optimization_barrier
    packed = jax.ShapeDtypeStruct
    whole = lambda *shape: pl.BlockSpec(shape, lambda i: (0,) * len(shape))
    far = pl.BlockSpec(memory_space=pltpu.HBM)
    states = cached_ssm_states.reshape(2, 64, 32, 128)
    sent1 = pl.pallas_call(
        pack_first,
        out_shape=packed((64, 32, 128), BF16),
        grid=(1,),
        in_specs=[smem()] * 4
        + [
            whole(64, 2048),
            whole(1, 64, 1024),
            whole(3, 2, 2048),
            whole(2, 3, 1, 2, 128),
            pl.BlockSpec((2, 64, 8, 128), lambda i: (0, 0, 3, 0)),
        ],
        out_specs=whole(64, 32, 128),
        compiler_params=params(60),
        cost_estimate=cost(0, 2 << 20),
        name="pack_first",
    )(
        tenant, tenant_adapter_row, cache_holder_index, cache_slot_index,
        jnp.swapaxes(adapter_down_panels, 1, 2).reshape(64, 2048), adapter_up_panels,
        jnp.swapaxes(inner_conv_cache, 0, 1), projection_conv_cache, states,
    )
    even = 1 - (lax.axis_index("head").astype(jnp.int32) & 1)
    cols = lambda *shape: pl.BlockSpec(shape, lambda i: (0,) * (len(shape) - 1) + (i,))
    scan_shapes = [
        packed((256, 2048), F32), packed((256, 2048), F32), packed((2048, 128), F32), packed((2048, 128), F32),
        packed((256, 128), BF16), packed((256, 128), BF16), packed((256, 128), F32), packed((32, 256), F32),
        packed((256, 128), F32), packed((32, 256), F32),
    ]
    wide_at = lambda *shape: pl.BlockSpec(shape, lambda i, on: (0, i * on[0]))
    tall_at = lambda *shape: pl.BlockSpec(shape, lambda i, on: (i * on[0], 0))
    fixed = lambda *shape: pl.BlockSpec(shape, lambda i, on: (0, 0))
    scan_specs = [
        wide_at(256, 256), wide_at(256, 256), tall_at(256, 128), tall_at(256, 128),
        fixed(256, 128), fixed(256, 128), fixed(256, 128), fixed(32, 256), fixed(256, 128), fixed(32, 256),
    ]
    scan_args = [
        inner_input, projection_input.reshape(256, 256), inner_conv_taps, projection_conv_taps.reshape(4, 256),
        step_before_bias.T, step_bias.reshape(1, 32), head_decay_rate.reshape(1, 32), head_skip_gain.reshape(1, 32),
    ]

    def scan(on, old, limit):
        inputs = [
            wide_at(256, 256), fixed(256, 256), wide_at(4, 256), fixed(4, 256), fixed(32, 256),
            fixed(1, 32), fixed(1, 32), fixed(1, 32),
        ]
        return pl.pallas_call(
            scan_kernel,
            out_shape=scan_shapes,
            grid_spec=pltpu.PrefetchScalarGridSpec(
                num_scalar_prefetch=1,
                grid=(8,),
                in_specs=inputs + scan_specs[: len(old)],
                out_specs=scan_specs,
                scratch_shapes=[pltpu.VMEM((264, 256), F32), pltpu.VMEM((264, 256), F32), pltpu.VMEM((256, 256), F32)],
            ),
            input_output_aliases={9 + i: i for i in range(len(old))},
            compiler_params=params(limit),
            cost_estimate=cost(2 << 30, 10 << 20),
            name="scan_late" if old else "scan_early",
        )(on.reshape(1), *scan_args, *old)

    early = scan(even, [], 60)
    sent1, *early = hold((sent1, *early))
    got1 = exchange(sent1, "req")
    late = scan(1 - even, early, 60)
    me = lax.axis_index("req").astype(jnp.int32).reshape(1)
    got1, me, *late = hold((got1, me, *late))
    part, gate, fresh, kept, c_main, b_main, decay, decay_t, step, step_t = late

    sent2, codes = pl.pallas_call(
        pack_second,
        out_shape=[packed((64, 56, 128), BF16), packed((8, 128), jnp.int32)],
        in_specs=[smem(), vmem(), pl.BlockSpec(memory_space=pl.ANY)],
        out_specs=[vmem(), smem()],
        scratch_shapes=[pltpu.VMEM((8, 128), jnp.int32), pltpu.SemaphoreType.DMA((2,))],
        compiler_params=params(52),
        cost_estimate=cost(0, 3 << 20),
        name="pack_second",
    )(me, got1, states)
    got2 = exchange(sent2, "req")
    sent3 = pl.pallas_call(
        pack_third,
        out_shape=packed((64, 32, 128), BF16),
        in_specs=[smem(), vmem(), vmem()],
        out_specs=vmem(),
        compiler_params=params(52),
        cost_estimate=cost(0, 1 << 20),
        name="pack_third",
    )(codes, got1, got2)
    sent3, got2 = hold((sent3, got2))
    got3 = exchange(sent3, "req")
    part, fresh, c_proj = pl.pallas_call(
        early_rows,
        out_shape=[packed((256, 2048), F32), packed((2048, 128), F32), packed((256, 128), BF16)],
        grid=(8,),
        in_specs=[
            pl.BlockSpec((16, 256), lambda i: (0, i)), whole(16, 256), cols(4, 256), whole(4, 256),
            pl.BlockSpec((64, 8, 128), lambda i: (0, 3, 0)),
            whole(1, 32), whole(256, 128), whole(256, 128), whole(32, 256), whole(256, 128), whole(32, 256),
            cols(256, 256), pl.BlockSpec((256, 128), lambda i: (i, 0)),
        ],
        out_specs=[cols(256, 256), pl.BlockSpec((256, 128), lambda i: (i, 0)), whole(256, 128)],
        scratch_shapes=[
            pltpu.VMEM((16, 256), F32), pltpu.VMEM((16, 256), F32),
            pltpu.VMEM((256, 128), F32), pltpu.VMEM((128, 128), BF16),
        ],
        compiler_params=params(52),
        cost_estimate=cost(1 << 29, 8 << 20),
        name="early_rows",
    )(
        inner_input, scan_args[1], inner_conv_taps, scan_args[3], got2, scan_args[7], c_main,
        decay, decay_t, step, step_t, part, fresh,
    )
    got3, part, c_proj, fresh = hold((got3, part, c_proj, fresh))

    normed, low = pl.pallas_call(
        state_kernel,
        out_shape=[packed((256, 2048), BF16), packed((8, 128, 128), BF16)],
        grid=(1,),
        in_specs=[whole(64, 32, 128), far, far, far, whole(1, 2048), whole(64, 56, 128)],
        out_specs=[whole(256, 2048), far],
        scratch_shapes=[pltpu.VMEM((256, 2048), F32)] * 3
        + [pltpu.VMEM((128, 128), BF16), pltpu.VMEM((256, 128), BF16), pltpu.SemaphoreType.DMA((2, 9))],
        compiler_params=params(52),
        cost_estimate=cost(1 << 28, 8 << 20),
        name="state",
    )(got3, c_proj, part, gate, group_norm_gain.reshape(1, 2048), got2)
    low, fresh = hold((low, fresh))
    parts = exchange(low, "head")
    updated = pl.pallas_call(
        update_kernel,
        out_shape=packed((1, 2048, 128), BF16),
        in_specs=[vmem()] * 3,
        out_specs=vmem(),
        compiler_params=params(),
        cost_estimate=cost(1 << 20, 3 << 20),
        name="update",
    )(got3, fresh, kept)
    parts, updated = hold((parts, updated))
    term = pl.pallas_call(
        up_kernel,
        out_shape=packed((256, 1024), BF16),
        in_specs=[vmem()] * 2,
        out_specs=vmem(),
        compiler_params=params(),
        cost_estimate=cost(1 << 26, 1 << 20),
        name="up",
    )(parts, got2)
    return normed, term, updated.reshape(1, 32, 64, 128)


def solution(mesh):
    return jax.shard_map(
        per_device,
        mesh=mesh,
        in_specs=(
            P("req", "head"),
            P("req", "head", None, None),
            P("req", "head"),
            P(None, "head"),
            P(None, "head", None, None),
            P("head"),
            P("head"),
            P("head"),
            P("head"),
            P("req"),
            P(),
            P("req"),
            P("req"),
            P("req", "head", None),
            P("req", None, "head"),
            P("req", "head", None, None),
            P("req", None, "head"),
            P("req", None, "head", None, None),
        ),
        out_specs=(P("req", "head"), P("req", "head"), P("req", "head", None, None)),
        check_vma=False,
    )
```

```python
import functools

import jax
import jax.numpy as jnp
from jax import lax
from jax.experimental import pallas as pl
from jax.experimental.pallas import tpu as pltpu
from jax.sharding import PartitionSpec as P

ADAPTER_SCALE = 2.0
NORM_EPSILON = 1e-05
F32, BF16 = jnp.float32, jnp.bfloat16
MIB = 1024 * 1024


def params(mib=20):
    return pltpu.CompilerParams(vmem_limit_bytes=mib * MIB)


def cost(flops, nbytes):
    return pl.CostEstimate(flops=flops, bytes_accessed=nbytes, transcendentals=0)


def smem():
    return pl.BlockSpec(memory_space=pltpu.SMEM)


def vmem():
    return pl.BlockSpec(memory_space=pltpu.VMEM)


def pack_first(tenant, table, owner, slot, down, up, convx, convbc, states, out):
    for chunk in range(64):
        col, row = chunk // 4, chunk % 4
        out[chunk, 0:16, :] = down[row * 16 : row * 16 + 16, col * 128 : col * 128 + 128]
        col, row = chunk // 8, chunk % 8
        out[chunk, 16:24, :] = up[0, row * 8 : row * 8 + 8, col * 128 : col * 128 + 128]
    lines = lax.broadcasted_iota(jnp.int32, (8, 128), 0)
    lanes = lax.broadcasted_iota(jnp.int32, (8, 128), 1)
    adapter = table[tenant[0]].astype(F32)
    base = jnp.where(lanes == 0, adapter, jnp.where(lanes == 1, owner[0].astype(F32), slot[0].astype(F32)))
    for chunk in range(64):
        tile = base
        if chunk < 54:
            for which in range(2):
                if chunk < 48:
                    k, col = chunk // 16, chunk % 16
                    line = convx[k, which : which + 1, col * 128 : col * 128 + 128]
                else:
                    k, side = (chunk - 48) // 2, (chunk - 48) % 2
                    line = convbc[which, k, 0, side : side + 1, :]
                tile = jnp.where(lines == which, jnp.broadcast_to(line.astype(F32), (8, 128)), tile)
        tile = jnp.where(lines >= 4, pltpu.roll(states[0, chunk].astype(F32), 6, 0), tile)
        tile = jnp.where(lines >= 6, states[1, chunk].astype(F32), tile)
        out[chunk, 24:32, :] = tile.astype(BF16)


def pack_second(me, first, states, out, codes, words, sems):
    lines = lax.broadcasted_iota(jnp.int32, (8, 128), 0)
    tall = lax.broadcasted_iota(jnp.int32, (64, 8, 128), 1)
    picked = jnp.sum(jnp.where(tall == 2, first[:, 24:32, :].astype(F32), 0.0), axis=1)
    turned = jnp.concatenate([picked, jnp.zeros((64, 128), F32)], axis=0).T
    words[...] = turned[0:8, :].astype(jnp.int32)
    to_scalars = pltpu.make_async_copy(words, codes, sems.at[0])
    to_scalars.start()
    to_scalars.wait()
    mine = lax.fori_loop(0, 64, lambda j, m: jnp.where(codes[1, j] == me[0], codes[2, j], m), 0, unroll=8)
    own = pltpu.make_async_copy(states.at[mine], out.at[:, 0:32, :], sems.at[1])
    own.start()

    def panels(j, carry):
        out[j, 32:56, :] = first[codes[0, j], 0:24, :]
        return carry

    lax.fori_loop(0, 64, panels, 0, unroll=8)
    own.wait()

    def lines_of(j, carry):
        tile = first[codes[1, j], 24:32, :].astype(F32)
        line = jnp.where(codes[2, j] == 0, tile[0:1], tile[1:2])
        out[j, 24:32, :] = jnp.where(lines == 6, line, out[j, 24:32, :].astype(F32)).astype(BF16)
        return carry

    lax.fori_loop(0, 64, lines_of, 0, unroll=8)


def pack_third(codes, first, second, out):
    lines = lax.broadcasted_iota(jnp.int32, (8, 128), 0)

    def body(j, carry):
        owner = codes[1, j]
        out[j, 0:24, :] = second[owner, 0:24, :]
        rest = first[owner, 24:32, :].astype(F32)
        rest = jnp.where(codes[2, j] == 0, pltpu.roll(rest, 2, 0), rest)
        out[j, 24:32, :] = jnp.where(lines >= 6, rest, second[owner, 24:32, :].astype(F32)).astype(BF16)
        return carry

    lax.fori_loop(0, 64, body, 0, unroll=8)


def silu(v):
    return v / (1.0 + jnp.exp(-v))


def history(convs, index):
    lines = lax.broadcasted_iota(jnp.int32, (8, 128), 0)
    old = [convs[i].astype(F32)[6:7, :] for i in index]
    return jnp.where(lines == 5, old[0], jnp.where(lines == 6, old[1], old[2]))


def conv(pad, taps, count):
    out = taps[0:1, :] * pad[5 : 5 + count, :]
    for k in range(1, 4):
        out = out + taps[k : k + 1, :] * pad[5 + k : 5 + count + k, :]
    return silu(out)


def conv_pair(pad, bc, taps, count):
    sides = []
    for side in range(2):
        at = slice(side * 128, side * 128 + 128)
        pad[8 : 8 + count, at] = bc[0:count, side, :].astype(F32)
        out = taps[0, side : side + 1, :] * pad[5 : 5 + count, at]
        for k in range(1, 4):
            out = out + taps[k, side : side + 1, :] * pad[5 + k : 5 + count + k, at]
        sides.append(silu(out))
    return jnp.concatenate(sides, axis=1)


def widened(value, lo, hi):
    left = lax.broadcasted_iota(jnp.int32, (value.shape[0], 128), 1) < 64
    return jnp.where(left, value[:, lo : lo + 1], value[:, hi : hi + 1])


def wide_row(row):
    return jnp.concatenate([row, jnp.zeros((1, 96), F32)], axis=1)


def dots(a, b, left, right):
    return lax.dot_general(a, b, (((left,), (right,)), ((), ())), preferred_element_type=F32)


def scan_kernel(flag, x, bc, taps, bc_taps, raw, bias, rate, skip, *rest):
    outs, (pad, pad_bc, score) = rest[-13:-3], rest[-3:]
    old = rest[:-13]
    part, gate, fresh, kept, c_out, b_out, decay, decay_t, step, step_t = outs
    block = pl.program_id(0)
    active = flag[0] == 1

    if old:

        @pl.when(jnp.logical_and(jnp.logical_not(active), block == 0))
        def _():
            for source, target in zip(old, outs):
                target[...] = source[...]

    @pl.when(jnp.logical_and(active, block == 0))
    def _():
        v = jnp.concatenate([raw[...].astype(F32), jnp.zeros((96, 256), F32)], axis=0).T + wide_row(bias[...])
        size = jnp.maximum(v, 0.0) + jnp.log(1.0 + jnp.exp(-jnp.abs(v)))
        drop = -wide_row(rate[...]) * size
        rows = lax.broadcasted_iota(jnp.int32, (256, 256), 0)
        cols = lax.broadcasted_iota(jnp.int32, (256, 256), 1)
        lower = (rows >= cols).astype(F32).astype(BF16)
        high = drop.astype(BF16)
        spare = drop - high.astype(F32)
        middle = spare.astype(BF16)
        low = (spare - middle.astype(F32)).astype(BF16)
        total = jnp.dot(lower, low, preferred_element_type=F32)
        total = total + jnp.dot(lower, middle, preferred_element_type=F32)
        total = total + jnp.dot(lower, high, preferred_element_type=F32)
        decay[...] = total
        step[...] = size
        decay_t[...] = total.T[0:32, :]
        step_t[...] = size.T[0:32, :]
        pad_bc[0:8, :] = jnp.zeros((8, 256), F32)
        both = jnp.where(rows >= 3, conv_pair(pad_bc, bc, bc_taps, 256), 0.0).astype(BF16)
        b_out[...] = both[:, 0:128]
        c_out[...] = both[:, 128:256]
        score[...] = dots(both[:, 128:256], both[:, 0:128], 1, 1)

    @pl.when(active)
    def _():
        pad[0:8, :] = jnp.zeros((8, 256), F32)
        pad[8:264, :] = x[...].astype(F32)
        tall = lax.broadcasted_iota(jnp.int32, (256, 256), 0)
        inner = jnp.where(tall >= 3, conv(pad, taps, 256), 0.0).astype(BF16)
        total = decay[...]
        shift = lax.rem(128 - 4 * block, 128)
        moved = pltpu.roll(total, shift, 1)
        grow = jnp.exp(moved)
        keep = pltpu.roll(jnp.exp(total[255:256, :] - total) * step[...], shift, 1)
        gains = pltpu.roll(jnp.broadcast_to(wide_row(skip[...]), (8, 128)), shift, 1)
        rows = lax.broadcasted_iota(jnp.int32, (128, 128), 0)
        cols = lax.broadcasted_iota(jnp.int32, (128, 128), 1)
        causal = rows >= cols
        left = cols < 64
        wide = inner.astype(F32)
        for pair in range(2):
            lo, hi = 2 * pair, 2 * pair + 1
            at = slice(pair * 128, pair * 128 + 128)
            values = inner[:, at]
            top, bottom = [], []
            for head in (lo, hi):
                here = moved[:, head : head + 1]
                there = decay_t[pl.ds(4 * block + head, 1), :]
                weight = step_t[pl.ds(4 * block + head, 1), :]
                gap = here[0:128] - there[:, 0:128]
                mix = score[0:128, 0:128] * jnp.exp(jnp.where(causal, gap, -jnp.inf)) * weight[:, 0:128]
                top.append(jnp.dot(mix.astype(BF16), values[0:128], preferred_element_type=F32))
                gap = here[128:256] - there[:, 0:128]
                mix = score[128:256, 0:128] * jnp.exp(gap) * weight[:, 0:128]
                early = mix.astype(BF16)
                gap = here[128:256] - there[:, 128:256]
                mix = score[128:256, 128:256] * jnp.exp(jnp.where(causal, gap, -jnp.inf)) * weight[:, 128:256]
                both = jnp.concatenate([early, mix.astype(BF16)], axis=1)
                bottom.append(jnp.dot(both, values, preferred_element_type=F32))
            gain = widened(gains[0:1, :], lo, hi)
            part[0:128, at] = jnp.where(left, top[0], top[1]) + gain * wide[0:128, at]
            part[128:256, at] = jnp.where(left, bottom[0], bottom[1]) + gain * wide[128:256, at]
            gate[:, at] = widened(grow, lo, hi)
            carried = (wide[:, at] * widened(keep, lo, hi)).astype(BF16)
            fresh[at, :] = dots(carried, b_out[...], 0, 0)
        for head in range(4):
            kept[head * 64 : head * 64 + 64, :] = jnp.broadcast_to(grow[255:256, head : head + 1], (64, 128))


def scan_first_kernel(flag, *refs):
    pack_refs, scan_refs, sent, scratch = refs[:9], refs[9:27], refs[27], refs[28:]

    @pl.when(pl.program_id(0) == 0)
    def _():
        pack_first(*pack_refs, sent)

    scan_kernel(flag, *scan_refs, *scratch)


def early_rows(
    x, bc, taps, bc_taps, convs, skip, c_main, decay, decay_t, step, step_t, part_in, fresh_in,
    part, fresh, c_out, pad, pad_bc, score, b_proj,
):
    block = pl.program_id(0)
    short = lax.broadcasted_iota(jnp.int32, (8, 256), 0) < 3
    rest = jnp.zeros((120, 128), F32)

    @pl.when(block == 0)
    def _():
        for side in range(2):
            at = slice(side * 128, side * 128 + 128)
            pad_bc[0:8, at] = history(convs, [48 + side, 50 + side, 52 + side])
        both = jnp.where(short, conv_pair(pad_bc, bc, bc_taps, 8), 0.0)
        b_proj[...] = jnp.concatenate([both[:, 0:128], rest], axis=0).astype(BF16)
        c_all = c_main[...].astype(F32)
        c_all = jnp.concatenate([c_all[0:8] + both[:, 128:256], c_all[8:256]], axis=0).astype(BF16)
        c_out[...] = c_all
        score[...] = dots(c_all, b_proj[...], 1, 1)

    for half in range(2):
        at = slice(half * 128, half * 128 + 128)
        col = block * 2 + half
        pad[0:8, at] = history(convs, [col, col + 16, col + 32])
    pad[8:16, :] = x[0:8, :].astype(F32)
    inner = jnp.where(short, conv(pad, taps, 8), 0.0).astype(BF16).astype(F32)
    total = decay[...]
    shift = lax.rem(128 - 4 * block, 128)
    moved = pltpu.roll(total, shift, 1)
    keep = pltpu.roll(jnp.exp(total[255:256, :] - total[0:8, :]) * step[0:8, :], shift, 1)
    gains = pltpu.roll(jnp.broadcast_to(wide_row(skip[...]), (8, 128)), shift, 1)
    rows = lax.broadcasted_iota(jnp.int32, (256, 128), 0)
    cols = lax.broadcasted_iota(jnp.int32, (256, 128), 1)
    causal = rows >= cols
    left = cols < 64
    for pair in range(2):
        lo, hi = 2 * pair, 2 * pair + 1
        at = slice(pair * 128, pair * 128 + 128)
        values = jnp.concatenate([inner[:, at], rest], axis=0).astype(BF16)
        added = []
        for head in (lo, hi):
            gap = moved[:, head : head + 1] - decay_t[pl.ds(4 * block + head, 1), :][:, 0:128]
            weight = step_t[pl.ds(4 * block + head, 1), :][:, 0:128]
            mix = score[...] * jnp.exp(jnp.where(causal, gap, -jnp.inf)) * weight
            added.append(jnp.dot(mix.astype(BF16), values, preferred_element_type=F32))
        part[:, at] = part_in[:, at] + jnp.where(left, added[0], added[1])
        part[0:8, at] = part[0:8, at] + widened(gains[0:1, :], lo, hi) * inner[:, at]
        carried = (inner[:, at] * widened(keep, lo, hi)).astype(BF16).astype(F32)
        carried = jnp.concatenate([carried, rest], axis=0).astype(BF16)
        fresh[at, :] = fresh_in[at, :] + dots(carried, b_proj[...], 0, 0)


def state_kernel(state, c_far, part_far, gate_far, gain, panels, normed, low, mixed, part, gate, tile, c_proj, sems):
    fetch = pltpu.make_async_copy(c_far, c_proj, sems.at[0, 8])
    fetch.start()
    copies = []
    for block in range(8):
        at = pl.ds(block * 256, 256)
        copies.append(pltpu.make_async_copy(part_far.at[:, at], part.at[:, at], sems.at[0, block]))
        copies.append(pltpu.make_async_copy(gate_far.at[:, at], gate.at[:, at], sems.at[1, block]))
    for copy in copies:
        copy.start()
    fetch.wait()
    c_value = c_proj[...]
    square = jnp.zeros((256, 128), F32)
    for block in range(8):
        at = slice(block * 256, block * 256 + 256)
        old = state[block * 8 : block * 8 + 8].reshape(256, 128)
        inter = lax.dot_general(c_value, old, (((1,), (1,)), ((), ())), preferred_element_type=F32)
        copies[2 * block].wait()
        copies[2 * block + 1].wait()
        total = part[:, at] + inter * gate[:, at]
        mixed[:, at] = total
        square = square + total[:, 0:128] * total[:, 0:128] + total[:, 128:256] * total[:, 128:256]
    mean = jnp.sum(square, axis=1, keepdims=True) * (1.0 / 2048.0)
    scale = lax.rsqrt(mean + NORM_EPSILON)
    acc = jnp.zeros((256, 64), F32)
    for col in range(16):
        at = slice(col * 128, col * 128 + 128)
        value = (mixed[:, at] * scale * gain[:, at]).astype(BF16)
        normed[:, at] = value
        panel = panels[col * 4 : col * 4 + 4, 32:48, :].reshape(64, 128)
        acc = acc + lax.dot_general(value, panel, (((1,), (1,)), ((), ())), preferred_element_type=F32)
    tile[...] = jnp.concatenate([acc[0:128], acc[128:256]], axis=1).astype(BF16)
    copies = [pltpu.make_async_copy(tile, low.at[peer], sems.at[0, peer]) for peer in range(8)]
    for copy in copies:
        copy.start()
    for copy in copies:
        copy.wait()


def update_kernel(state, fresh, kept, updated):
    updated[0] = (fresh[...] + kept[...] * state[...].reshape(2048, 128).astype(F32)).astype(BF16)


def up_kernel(parts, up, out):
    total = parts[0].astype(F32)
    for peer in range(1, 8):
        total = total + parts[peer].astype(F32)
    reduced = total.astype(BF16)
    halves = [reduced[:, 0:64], reduced[:, 64:128]]
    for col in range(8):
        panel = up[col * 8 : col * 8 + 8, 48:56, :].astype(F32).reshape(64, 128).astype(BF16)
        at = slice(col * 128, col * 128 + 128)
        for half in range(2):
            value = jnp.dot(halves[half], panel, preferred_element_type=F32) * ADAPTER_SCALE
            out[half * 128 : half * 128 + 128, at] = value.astype(BF16)


def exchange(value, axis):
    return lax.all_to_all(value, axis, split_axis=0, concat_axis=0, tiled=True)


def per_device(
    inner_input,
    projection_input,
    step_before_bias,
    inner_conv_taps,
    projection_conv_taps,
    step_bias,
    head_decay_rate,
    head_skip_gain,
    group_norm_gain,
    tenant,
    tenant_adapter_row,
    cache_holder_index,
    cache_slot_index,
    adapter_down_panels,
    adapter_up_panels,
    cached_ssm_states,
    inner_conv_cache,
    projection_conv_cache,
):
    hold = lax.optimization_barrier
    packed = jax.ShapeDtypeStruct
    whole = lambda *shape: pl.BlockSpec(shape, lambda i: (0,) * len(shape))
    far = pl.BlockSpec(memory_space=pltpu.HBM)
    states = cached_ssm_states.reshape(2, 64, 32, 128)
    pack_args = [
        tenant, tenant_adapter_row, cache_holder_index, cache_slot_index,
        jnp.swapaxes(adapter_down_panels, 1, 2).reshape(64, 2048), adapter_up_panels,
        jnp.swapaxes(inner_conv_cache, 0, 1), projection_conv_cache, states,
    ]
    even = 1 - (lax.axis_index("head").astype(jnp.int32) & 1)
    cols = lambda *shape: pl.BlockSpec(shape, lambda i: (0,) * (len(shape) - 1) + (i,))
    scan_shapes = [
        packed((256, 2048), F32), packed((256, 2048), F32), packed((2048, 128), F32), packed((2048, 128), F32),
        packed((256, 128), BF16), packed((256, 128), BF16), packed((256, 128), F32), packed((32, 256), F32),
        packed((256, 128), F32), packed((32, 256), F32),
    ]
    wide_at = lambda *shape: pl.BlockSpec(shape, lambda i, on: (0, i * on[0]))
    tall_at = lambda *shape: pl.BlockSpec(shape, lambda i, on: (i * on[0], 0))
    fixed = lambda *shape: pl.BlockSpec(shape, lambda i, on: (0,) * len(shape))
    scan_specs = [
        wide_at(256, 256), wide_at(256, 256), tall_at(256, 128), tall_at(256, 128),
        fixed(256, 128), fixed(256, 128), fixed(256, 128), fixed(32, 256), fixed(256, 128), fixed(32, 256),
    ]
    scan_args = [
        inner_input, projection_input.reshape(256, 2, 128), inner_conv_taps, projection_conv_taps.reshape(4, 2, 128),
        step_before_bias.T, step_bias.reshape(1, 32), head_decay_rate.reshape(1, 32), head_skip_gain.reshape(1, 32),
    ]

    pack_specs = [smem()] * 4 + [
        fixed(64, 2048), fixed(1, 64, 1024), fixed(3, 2, 2048), fixed(2, 3, 1, 2, 128),
        pl.BlockSpec((2, 64, 8, 128), lambda i, on: (0, 0, 3, 0)),
    ]

    def scan(on, old, limit):
        inputs = [
            wide_at(256, 256), fixed(256, 2, 128), wide_at(4, 256), fixed(4, 2, 128), fixed(32, 256),
            fixed(1, 32), fixed(1, 32), fixed(1, 32),
        ]
        first = not old
        return pl.pallas_call(
            scan_first_kernel if first else scan_kernel,
            out_shape=scan_shapes + [packed((64, 32, 128), BF16)] * first,
            grid_spec=pltpu.PrefetchScalarGridSpec(
                num_scalar_prefetch=1,
                grid=(8,),
                in_specs=pack_specs * first + inputs + scan_specs[: len(old)],
                out_specs=scan_specs + [fixed(64, 32, 128)] * first,
                scratch_shapes=[pltpu.VMEM((264, 256), F32), pltpu.VMEM((264, 256), F32), pltpu.VMEM((256, 256), F32)],
            ),
            input_output_aliases={9 + i: i for i in range(len(old))},
            compiler_params=params(limit),
            cost_estimate=cost(2 << 30, 10 << 20),
            name="scan_early" if first else "scan_late",
        )(on.reshape(1), *(pack_args * first), *scan_args, *old)

    *early, sent1 = scan(even, [], 60)
    sent1, *early = hold((sent1, *early))
    got1 = exchange(sent1, "req")
    late = scan(1 - even, early, 60)
    me = lax.axis_index("req").astype(jnp.int32).reshape(1)
    got1, me, *late = hold((got1, me, *late))
    part, gate, fresh, kept, c_main, b_main, decay, decay_t, step, step_t = late

    sent2, codes = pl.pallas_call(
        pack_second,
        out_shape=[packed((64, 56, 128), BF16), packed((8, 128), jnp.int32)],
        in_specs=[smem(), vmem(), pl.BlockSpec(memory_space=pl.ANY)],
        out_specs=[vmem(), smem()],
        scratch_shapes=[pltpu.VMEM((8, 128), jnp.int32), pltpu.SemaphoreType.DMA((2,))],
        compiler_params=params(52),
        cost_estimate=cost(0, 3 << 20),
        name="pack_second",
    )(me, got1, states)
    got2 = exchange(sent2, "req")
    sent3 = pl.pallas_call(
        pack_third,
        out_shape=packed((64, 32, 128), BF16),
        in_specs=[smem(), vmem(), vmem()],
        out_specs=vmem(),
        compiler_params=params(52),
        cost_estimate=cost(0, 1 << 20),
        name="pack_third",
    )(codes, got1, got2)
    sent3, got2 = hold((sent3, got2))
    got3 = exchange(sent3, "req")
    part, fresh, c_proj = pl.pallas_call(
        early_rows,
        out_shape=[packed((256, 2048), F32), packed((2048, 128), F32), packed((256, 128), BF16)],
        grid=(8,),
        in_specs=[
            pl.BlockSpec((16, 256), lambda i: (0, i)), whole(16, 2, 128), cols(4, 256), whole(4, 2, 128),
            pl.BlockSpec((64, 8, 128), lambda i: (0, 3, 0)),
            whole(1, 32), whole(256, 128), whole(256, 128), whole(32, 256), whole(256, 128), whole(32, 256),
            cols(256, 256), pl.BlockSpec((256, 128), lambda i: (i, 0)),
        ],
        out_specs=[cols(256, 256), pl.BlockSpec((256, 128), lambda i: (i, 0)), whole(256, 128)],
        scratch_shapes=[
            pltpu.VMEM((16, 256), F32), pltpu.VMEM((16, 256), F32),
            pltpu.VMEM((256, 128), F32), pltpu.VMEM((128, 128), BF16),
        ],
        compiler_params=params(52),
        cost_estimate=cost(1 << 29, 8 << 20),
        name="early_rows",
    )(
        inner_input, scan_args[1], inner_conv_taps, scan_args[3], got2, scan_args[7], c_main,
        decay, decay_t, step, step_t, part, fresh,
    )
    got3, part, c_proj, fresh = hold((got3, part, c_proj, fresh))

    normed, low = pl.pallas_call(
        state_kernel,
        out_shape=[packed((256, 2048), BF16), packed((8, 128, 128), BF16)],
        grid=(1,),
        in_specs=[whole(64, 32, 128), far, far, far, whole(1, 2048), whole(64, 56, 128)],
        out_specs=[whole(256, 2048), far],
        scratch_shapes=[pltpu.VMEM((256, 2048), F32)] * 3
        + [pltpu.VMEM((128, 128), BF16), pltpu.VMEM((256, 128), BF16), pltpu.SemaphoreType.DMA((2, 9))],
        compiler_params=params(52),
        cost_estimate=cost(1 << 28, 8 << 20),
        name="state",
    )(got3, c_proj, part, gate, group_norm_gain.reshape(1, 2048), got2)
    low, fresh = hold((low, fresh))
    parts = exchange(low, "head")
    updated = pl.pallas_call(
        update_kernel,
        out_shape=packed((1, 2048, 128), BF16),
        in_specs=[vmem()] * 3,
        out_specs=vmem(),
        compiler_params=params(),
        cost_estimate=cost(1 << 20, 3 << 20),
        name="update",
    )(got3, fresh, kept)
    parts, updated = hold((parts, updated))
    term = pl.pallas_call(
        up_kernel,
        out_shape=packed((256, 1024), BF16),
        in_specs=[vmem()] * 2,
        out_specs=vmem(),
        compiler_params=params(),
        cost_estimate=cost(1 << 26, 1 << 20),
        name="up",
    )(parts, got2)
    return normed, term, updated.reshape(1, 32, 64, 128)


def solution(mesh):
    return jax.shard_map(
        per_device,
        mesh=mesh,
        in_specs=(
            P("req", "head"),
            P("req", "head", None, None),
            P("req", "head"),
            P(None, "head"),
            P(None, "head", None, None),
            P("head"),
            P("head"),
            P("head"),
            P("head"),
            P("req"),
            P(),
            P("req"),
            P("req"),
            P("req", "head", None),
            P("req", None, "head"),
            P("req", "head", None, None),
            P("req", None, "head"),
            P("req", None, "head", None, None),
        ),
        out_specs=(P("req", "head"), P("req", "head"), P("req", "head", None, None)),
        check_vma=False,
    )
```

```python
import functools

import jax
import jax.numpy as jnp
from jax import lax
from jax.experimental import pallas as pl
from jax.experimental.pallas import tpu as pltpu
from jax.sharding import PartitionSpec as P

ADAPTER_SCALE = 2.0
NORM_EPSILON = 1e-05
F32, BF16 = jnp.float32, jnp.bfloat16
MIB = 1024 * 1024


def params(mib=20):
    return pltpu.CompilerParams(vmem_limit_bytes=mib * MIB)


def cost(flops, nbytes):
    return pl.CostEstimate(flops=flops, bytes_accessed=nbytes, transcendentals=0)


def smem():
    return pl.BlockSpec(memory_space=pltpu.SMEM)


def vmem():
    return pl.BlockSpec(memory_space=pltpu.VMEM)


def pack_first(tenant, table, owner, slot, down, up, convx, convbc, states, out):
    for chunk in range(64):
        col, row = chunk // 4, chunk % 4
        out[chunk, 0:16, :] = down[row * 16 : row * 16 + 16, col * 128 : col * 128 + 128]
        col, row = chunk // 8, chunk % 8
        out[chunk, 16:24, :] = up[0, row * 8 : row * 8 + 8, col * 128 : col * 128 + 128]
    lines = lax.broadcasted_iota(jnp.int32, (8, 128), 0)
    lanes = lax.broadcasted_iota(jnp.int32, (8, 128), 1)
    adapter = table[tenant[0]].astype(F32)
    base = jnp.where(lanes == 0, adapter, jnp.where(lanes == 1, owner[0].astype(F32), slot[0].astype(F32)))
    for chunk in range(64):
        tile = base
        if chunk < 54:
            for which in range(2):
                if chunk < 48:
                    k, col = chunk // 16, chunk % 16
                    line = convx[k, which : which + 1, col * 128 : col * 128 + 128]
                else:
                    k, side = (chunk - 48) // 2, (chunk - 48) % 2
                    line = convbc[which, k, 0, side : side + 1, :]
                tile = jnp.where(lines == which, jnp.broadcast_to(line.astype(F32), (8, 128)), tile)
        tile = jnp.where(lines >= 4, pltpu.roll(states[0, chunk].astype(F32), 6, 0), tile)
        tile = jnp.where(lines >= 6, states[1, chunk].astype(F32), tile)
        out[chunk, 24:32, :] = tile.astype(BF16)


def pack_second(me, first, states, out, codes, words, sems):
    lines = lax.broadcasted_iota(jnp.int32, (8, 128), 0)
    tall = lax.broadcasted_iota(jnp.int32, (64, 8, 128), 1)
    picked = jnp.sum(jnp.where(tall == 2, first[:, 24:32, :].astype(F32), 0.0), axis=1)
    turned = jnp.concatenate([picked, jnp.zeros((64, 128), F32)], axis=0).T
    words[...] = turned[0:8, :].astype(jnp.int32)
    to_scalars = pltpu.make_async_copy(words, codes, sems.at[0])
    to_scalars.start()
    to_scalars.wait()
    mine = lax.fori_loop(0, 64, lambda j, m: jnp.where(codes[1, j] == me[0], codes[2, j], m), 0, unroll=8)
    own = pltpu.make_async_copy(states.at[mine], out.at[:, 0:32, :], sems.at[1])
    own.start()

    def panels(j, carry):
        out[j, 32:56, :] = first[codes[0, j], 0:24, :]
        return carry

    lax.fori_loop(0, 64, panels, 0, unroll=8)
    own.wait()

    def lines_of(j, carry):
        tile = first[codes[1, j], 24:32, :].astype(F32)
        line = jnp.where(codes[2, j] == 0, tile[0:1], tile[1:2])
        out[j, 24:32, :] = jnp.where(lines == 6, line, out[j, 24:32, :].astype(F32)).astype(BF16)
        return carry

    lax.fori_loop(0, 64, lines_of, 0, unroll=8)


def pack_third(codes, first, second, out):
    lines = lax.broadcasted_iota(jnp.int32, (8, 128), 0)

    def body(j, carry):
        owner = codes[1, j]
        out[j, 0:24, :] = second[owner, 0:24, :]
        rest = first[owner, 24:32, :].astype(F32)
        rest = jnp.where(codes[2, j] == 0, pltpu.roll(rest, 2, 0), rest)
        out[j, 24:32, :] = jnp.where(lines >= 6, rest, second[owner, 24:32, :].astype(F32)).astype(BF16)
        return carry

    lax.fori_loop(0, 64, body, 0, unroll=8)


def silu(v):
    return v / (1.0 + jnp.exp(-v))


def history(convs, index):
    lines = lax.broadcasted_iota(jnp.int32, (8, 128), 0)
    old = [convs[i].astype(F32)[6:7, :] for i in index]
    return jnp.where(lines == 5, old[0], jnp.where(lines == 6, old[1], old[2]))


def conv(pad, taps, count):
    out = taps[0:1, :] * pad[5 : 5 + count, :]
    for k in range(1, 4):
        out = out + taps[k : k + 1, :] * pad[5 + k : 5 + count + k, :]
    return silu(out)


def conv_pair(pad, bc, taps, count):
    sides = []
    for side in range(2):
        at = slice(side * 128, side * 128 + 128)
        pad[8 : 8 + count, at] = bc[0:count, side, :].astype(F32)
        out = taps[0, side : side + 1, :] * pad[5 : 5 + count, at]
        for k in range(1, 4):
            out = out + taps[k, side : side + 1, :] * pad[5 + k : 5 + count + k, at]
        sides.append(silu(out))
    return jnp.concatenate(sides, axis=1)


def widened(value, lo, hi):
    left = lax.broadcasted_iota(jnp.int32, (value.shape[0], 128), 1) < 64
    return jnp.where(left, value[:, lo : lo + 1], value[:, hi : hi + 1])


def wide_row(row):
    return jnp.concatenate([row, jnp.zeros((1, 96), F32)], axis=1)


def dots(a, b, left, right):
    return lax.dot_general(a, b, (((left,), (right,)), ((), ())), preferred_element_type=F32)


def scan_kernel(flag, x, bc, taps, bc_taps, raw, bias, rate, skip, *rest):
    outs, (pad, pad_bc, score) = rest[-13:-3], rest[-3:]
    old = rest[:-13]
    part, gate, fresh, kept, c_out, b_out, decay, decay_t, step, step_t = outs
    block = pl.program_id(0)
    active = flag[0] == 1

    if old:

        @pl.when(jnp.logical_and(jnp.logical_not(active), block == 0))
        def _():
            for source, target in zip(old, outs):
                target[...] = source[...]

    @pl.when(jnp.logical_and(active, block == 0))
    def _():
        v = jnp.concatenate([raw[...].astype(F32), jnp.zeros((96, 256), F32)], axis=0).T + wide_row(bias[...])
        size = jnp.maximum(v, 0.0) + jnp.log(1.0 + jnp.exp(-jnp.abs(v)))
        drop = -wide_row(rate[...]) * size
        rows = lax.broadcasted_iota(jnp.int32, (256, 256), 0)
        cols = lax.broadcasted_iota(jnp.int32, (256, 256), 1)
        lower = (rows >= cols).astype(F32).astype(BF16)
        high = drop.astype(BF16)
        spare = drop - high.astype(F32)
        middle = spare.astype(BF16)
        low = (spare - middle.astype(F32)).astype(BF16)
        total = jnp.dot(lower, low, preferred_element_type=F32)
        total = total + jnp.dot(lower, middle, preferred_element_type=F32)
        total = total + jnp.dot(lower, high, preferred_element_type=F32)
        decay[...] = total
        step[...] = size
        decay_t[...] = total.T[0:32, :]
        step_t[...] = size.T[0:32, :]
        pad_bc[0:8, :] = jnp.zeros((8, 256), F32)
        both = jnp.where(rows >= 3, conv_pair(pad_bc, bc, bc_taps, 256), 0.0).astype(BF16)
        b_out[...] = both[:, 0:128]
        c_out[...] = both[:, 128:256]
        score[...] = dots(both[:, 128:256], both[:, 0:128], 1, 1)

    @pl.when(active)
    def _():
        pad[0:8, :] = jnp.zeros((8, 256), F32)
        pad[8:264, :] = x[...].astype(F32)
        tall = lax.broadcasted_iota(jnp.int32, (256, 256), 0)
        inner = jnp.where(tall >= 3, conv(pad, taps, 256), 0.0).astype(BF16)
        total = decay[...]
        shift = lax.rem(128 - 4 * block, 128)
        moved = pltpu.roll(total, shift, 1)
        grow = jnp.exp(moved)
        keep = pltpu.roll(jnp.exp(total[255:256, :] - total) * step[...], shift, 1)
        gains = pltpu.roll(jnp.broadcast_to(wide_row(skip[...]), (8, 128)), shift, 1)
        rows = lax.broadcasted_iota(jnp.int32, (128, 128), 0)
        cols = lax.broadcasted_iota(jnp.int32, (128, 128), 1)
        causal = rows >= cols
        left = cols < 64
        wide = inner.astype(F32)
        for pair in range(2):
            lo, hi = 2 * pair, 2 * pair + 1
            at = slice(pair * 128, pair * 128 + 128)
            values = inner[:, at]
            top, bottom = [], []
            for head in (lo, hi):
                here = moved[:, head : head + 1]
                there = decay_t[pl.ds(4 * block + head, 1), :]
                weight = step_t[pl.ds(4 * block + head, 1), :]
                gap = here[0:128] - there[:, 0:128]
                mix = score[0:128, 0:128] * jnp.exp(jnp.where(causal, gap, -jnp.inf)) * weight[:, 0:128]
                top.append(jnp.dot(mix.astype(BF16), values[0:128], preferred_element_type=F32))
                gap = here[128:256] - there[:, 0:128]
                mix = score[128:256, 0:128] * jnp.exp(gap) * weight[:, 0:128]
                early = mix.astype(BF16)
                gap = here[128:256] - there[:, 128:256]
                mix = score[128:256, 128:256] * jnp.exp(jnp.where(causal, gap, -jnp.inf)) * weight[:, 128:256]
                both = jnp.concatenate([early, mix.astype(BF16)], axis=1)
                bottom.append(jnp.dot(both, values, preferred_element_type=F32))
            gain = widened(gains[0:1, :], lo, hi)
            part[0:128, at] = jnp.where(left, top[0], top[1]) + gain * wide[0:128, at]
            part[128:256, at] = jnp.where(left, bottom[0], bottom[1]) + gain * wide[128:256, at]
            gate[:, at] = widened(grow, lo, hi)
            carried = (wide[:, at] * widened(keep, lo, hi)).astype(BF16)
            fresh[at, :] = dots(carried, b_out[...], 0, 0)
        for head in range(4):
            kept[head * 64 : head * 64 + 64, :] = jnp.broadcast_to(grow[255:256, head : head + 1], (64, 128))


def scan_first_kernel(flag, *refs):
    pack_refs, scan_refs, sent, scratch = refs[:9], refs[9:27], refs[27], refs[28:]

    @pl.when(pl.program_id(0) == 0)
    def _():
        pack_first(*pack_refs, sent)

    scan_kernel(flag, *scan_refs, *scratch)


def early_rows(
    x, bc, taps, bc_taps, convs, skip, c_main, decay, decay_t, step, step_t, part_in, fresh_in,
    part, fresh, pad, pad_bc, score, b_proj, c_all,
):
    block = pl.program_id(0)

    @pl.when(block == 8)
    def _():
        part[:, 0:128] = c_all[...].astype(F32)

    @pl.when(block < 8)
    def _():
        early_block(
            block, x, bc, taps, bc_taps, convs, skip, c_main, decay, decay_t, step, step_t, part_in, fresh_in,
            part, fresh, pad, pad_bc, score, b_proj, c_all,
        )


def early_block(
    block, x, bc, taps, bc_taps, convs, skip, c_main, decay, decay_t, step, step_t, part_in, fresh_in,
    part, fresh, pad, pad_bc, score, b_proj, c_proj,
):
    short = lax.broadcasted_iota(jnp.int32, (8, 256), 0) < 3
    rest = jnp.zeros((120, 128), F32)

    @pl.when(block == 0)
    def _():
        for side in range(2):
            at = slice(side * 128, side * 128 + 128)
            pad_bc[0:8, at] = history(convs, [48 + side, 50 + side, 52 + side])
        both = jnp.where(short, conv_pair(pad_bc, bc, bc_taps, 8), 0.0)
        b_proj[...] = jnp.concatenate([both[:, 0:128], rest], axis=0).astype(BF16)
        c_all = c_main[...].astype(F32)
        c_all = jnp.concatenate([c_all[0:8] + both[:, 128:256], c_all[8:256]], axis=0).astype(BF16)
        c_proj[...] = c_all
        score[...] = dots(c_all, b_proj[...], 1, 1)

    for half in range(2):
        at = slice(half * 128, half * 128 + 128)
        col = block * 2 + half
        pad[0:8, at] = history(convs, [col, col + 16, col + 32])
    pad[8:16, :] = x[0:8, :].astype(F32)
    inner = jnp.where(short, conv(pad, taps, 8), 0.0).astype(BF16).astype(F32)
    total = decay[...]
    shift = lax.rem(128 - 4 * block, 128)
    moved = pltpu.roll(total, shift, 1)
    keep = pltpu.roll(jnp.exp(total[255:256, :] - total[0:8, :]) * step[0:8, :], shift, 1)
    gains = pltpu.roll(jnp.broadcast_to(wide_row(skip[...]), (8, 128)), shift, 1)
    rows = lax.broadcasted_iota(jnp.int32, (256, 128), 0)
    cols = lax.broadcasted_iota(jnp.int32, (256, 128), 1)
    causal = rows >= cols
    left = cols < 64
    for pair in range(2):
        lo, hi = 2 * pair, 2 * pair + 1
        at = slice(pair * 128, pair * 128 + 128)
        values = jnp.concatenate([inner[:, at], rest], axis=0).astype(BF16)
        added = []
        for head in (lo, hi):
            gap = moved[:, head : head + 1] - decay_t[pl.ds(4 * block + head, 1), :][:, 0:128]
            weight = step_t[pl.ds(4 * block + head, 1), :][:, 0:128]
            mix = score[...] * jnp.exp(jnp.where(causal, gap, -jnp.inf)) * weight
            added.append(jnp.dot(mix.astype(BF16), values, preferred_element_type=F32))
        part[:, at] = part_in[:, at] + jnp.where(left, added[0], added[1])
        part[0:8, at] = part[0:8, at] + widened(gains[0:1, :], lo, hi) * inner[:, at]
        carried = (inner[:, at] * widened(keep, lo, hi)).astype(BF16).astype(F32)
        carried = jnp.concatenate([carried, rest], axis=0).astype(BF16)
        fresh[at, :] = fresh_in[at, :] + dots(carried, b_proj[...], 0, 0)


def state_kernel(state, part_far, gate_far, gain, panels, normed_far, low, mixed, part, gate, tile, c_proj, normed, sems):
    fetch = pltpu.make_async_copy(part_far.at[:, pl.ds(2048, 128)], c_proj, sems.at[0, 8])
    fetch.start()
    copies = []
    for block in range(8):
        at = pl.ds(block * 256, 256)
        copies.append(pltpu.make_async_copy(part_far.at[:, at], part.at[:, at], sems.at[0, block]))
        copies.append(pltpu.make_async_copy(gate_far.at[:, at], gate.at[:, at], sems.at[1, block]))
    for copy in copies:
        copy.start()
    fetch.wait()
    c_value = c_proj[...].astype(BF16)
    square = jnp.zeros((256, 128), F32)
    for block in range(8):
        at = slice(block * 256, block * 256 + 256)
        old = state[block * 8 : block * 8 + 8].reshape(256, 128)
        inter = lax.dot_general(c_value, old, (((1,), (1,)), ((), ())), preferred_element_type=F32)
        copies[2 * block].wait()
        copies[2 * block + 1].wait()
        total = part[:, at] + inter * gate[:, at]
        mixed[:, at] = total
        square = square + total[:, 0:128] * total[:, 0:128] + total[:, 128:256] * total[:, 128:256]
    mean = jnp.sum(square, axis=1, keepdims=True) * (1.0 / 2048.0)
    scale = lax.rsqrt(mean + NORM_EPSILON)
    acc = jnp.zeros((256, 64), F32)
    leaving = []
    for col in range(16):
        at = slice(col * 128, col * 128 + 128)
        value = (mixed[:, at] * scale * gain[:, at]).astype(BF16)
        normed[:, at] = value
        panel = panels[col * 4 : col * 4 + 4, 32:48, :].reshape(64, 128)
        acc = acc + lax.dot_general(value, panel, (((1,), (1,)), ((), ())), preferred_element_type=F32)
        if col % 4 == 3:
            at = pl.ds(col * 128 - 384, 512)
            leaving.append(pltpu.make_async_copy(normed.at[:, at], normed_far.at[:, at], sems.at[1, col // 4]))
            leaving[-1].start()
    tile[...] = jnp.concatenate([acc[0:128], acc[128:256]], axis=1).astype(BF16)
    copies = [pltpu.make_async_copy(tile, low.at[peer], sems.at[0, peer]) for peer in range(8)]
    for copy in copies:
        copy.start()
    for copy in copies + leaving:
        copy.wait()


def update_kernel(state, fresh, kept, updated):
    updated[0] = (fresh[...] + kept[...] * state[...].reshape(2048, 128).astype(F32)).astype(BF16)


def up_kernel(parts, up, out):
    total = parts[0].astype(F32)
    for peer in range(1, 8):
        total = total + parts[peer].astype(F32)
    reduced = total.astype(BF16)
    halves = [reduced[:, 0:64], reduced[:, 64:128]]
    for col in range(8):
        panel = up[col * 8 : col * 8 + 8, 48:56, :].astype(F32).reshape(64, 128).astype(BF16)
        at = slice(col * 128, col * 128 + 128)
        for half in range(2):
            value = jnp.dot(halves[half], panel, preferred_element_type=F32) * ADAPTER_SCALE
            out[half * 128 : half * 128 + 128, at] = value.astype(BF16)


def exchange(value, axis):
    return lax.all_to_all(value, axis, split_axis=0, concat_axis=0, tiled=True)


def per_device(
    inner_input,
    projection_input,
    step_before_bias,
    inner_conv_taps,
    projection_conv_taps,
    step_bias,
    head_decay_rate,
    head_skip_gain,
    group_norm_gain,
    tenant,
    tenant_adapter_row,
    cache_holder_index,
    cache_slot_index,
    adapter_down_panels,
    adapter_up_panels,
    cached_ssm_states,
    inner_conv_cache,
    projection_conv_cache,
):
    hold = lax.optimization_barrier
    packed = jax.ShapeDtypeStruct
    whole = lambda *shape: pl.BlockSpec(shape, lambda i: (0,) * len(shape))
    far = pl.BlockSpec(memory_space=pltpu.HBM)
    states = cached_ssm_states.reshape(2, 64, 32, 128)
    pack_args = [
        tenant, tenant_adapter_row, cache_holder_index, cache_slot_index,
        jnp.swapaxes(adapter_down_panels, 1, 2).reshape(64, 2048), adapter_up_panels,
        jnp.swapaxes(inner_conv_cache, 0, 1), projection_conv_cache, states,
    ]
    even = 1 - (lax.axis_index("head").astype(jnp.int32) & 1)
    cols = lambda *shape: pl.BlockSpec(shape, lambda i: (0,) * (len(shape) - 1) + (i,))
    scan_shapes = [
        packed((256, 2048), F32), packed((256, 2048), F32), packed((2048, 128), F32), packed((2048, 128), F32),
        packed((256, 128), BF16), packed((256, 128), BF16), packed((256, 128), F32), packed((32, 256), F32),
        packed((256, 128), F32), packed((32, 256), F32),
    ]
    wide_at = lambda *shape: pl.BlockSpec(shape, lambda i, on: (0, i * on[0]))
    tall_at = lambda *shape: pl.BlockSpec(shape, lambda i, on: (i * on[0], 0))
    fixed = lambda *shape: pl.BlockSpec(shape, lambda i, on: (0,) * len(shape))
    scan_specs = [
        wide_at(256, 256), wide_at(256, 256), tall_at(256, 128), tall_at(256, 128),
        fixed(256, 128), fixed(256, 128), fixed(256, 128), fixed(32, 256), fixed(256, 128), fixed(32, 256),
    ]
    scan_args = [
        inner_input, projection_input.reshape(256, 2, 128), inner_conv_taps, projection_conv_taps.reshape(4, 2, 128),
        step_before_bias.T, step_bias.reshape(1, 32), head_decay_rate.reshape(1, 32), head_skip_gain.reshape(1, 32),
    ]

    sent1 = pl.pallas_call(
        pack_first,
        out_shape=packed((64, 32, 128), BF16),
        grid=(1,),
        in_specs=[smem()] * 4
        + [
            whole(64, 2048), whole(1, 64, 1024), whole(3, 2, 2048), whole(2, 3, 1, 2, 128),
            pl.BlockSpec((2, 64, 8, 128), lambda i: (0, 0, 3, 0)),
        ],
        out_specs=whole(64, 32, 128),
        compiler_params=params(60),
        cost_estimate=cost(0, 2 << 20),
        name="pack_first",
    )(*pack_args)

    def scan(on, old, limit):
        inputs = [
            wide_at(256, 256), fixed(256, 2, 128), wide_at(4, 256), fixed(4, 2, 128), fixed(32, 256),
            fixed(1, 32), fixed(1, 32), fixed(1, 32),
        ]
        first, pack_specs = False, []
        return pl.pallas_call(
            scan_first_kernel if first else scan_kernel,
            out_shape=scan_shapes + [packed((64, 32, 128), BF16)] * first,
            grid_spec=pltpu.PrefetchScalarGridSpec(
                num_scalar_prefetch=1,
                grid=(8,),
                in_specs=pack_specs * first + inputs + scan_specs[: len(old)],
                out_specs=scan_specs + [fixed(64, 32, 128)] * first,
                scratch_shapes=[pltpu.VMEM((264, 256), F32), pltpu.VMEM((264, 256), F32), pltpu.VMEM((256, 256), F32)],
            ),
            input_output_aliases={9 + i: i for i in range(len(old))},
            compiler_params=params(limit),
            cost_estimate=cost(2 << 30, 10 << 20),
            name="scan_late" if old else "scan_early",
        )(on.reshape(1), *(pack_args * first), *scan_args, *old)

    skipped = pl.pallas_call(
        lambda *refs: None, out_shape=scan_shapes, out_specs=[far] * 10, compiler_params=params(60), name="skip"
    )
    early = lax.cond(even == 1, lambda: scan(jnp.int32(1), [], 60), lambda: skipped())
    sent1, *early = hold((sent1, *early))
    got1 = exchange(sent1, "req")
    late = scan(1 - even, early, 60)
    me = lax.axis_index("req").astype(jnp.int32).reshape(1)
    got1, me, *late = hold((got1, me, *late))
    part, gate, fresh, kept, c_main, b_main, decay, decay_t, step, step_t = late

    sent2, codes = pl.pallas_call(
        pack_second,
        out_shape=[packed((64, 56, 128), BF16), packed((8, 128), jnp.int32)],
        in_specs=[smem(), vmem(), pl.BlockSpec(memory_space=pl.ANY)],
        out_specs=[vmem(), smem()],
        scratch_shapes=[pltpu.VMEM((8, 128), jnp.int32), pltpu.SemaphoreType.DMA((2,))],
        compiler_params=params(52),
        cost_estimate=cost(0, 3 << 20),
        name="pack_second",
    )(me, got1, states)
    got2 = exchange(sent2, "req")
    sent3 = pl.pallas_call(
        pack_third,
        out_shape=packed((64, 32, 128), BF16),
        in_specs=[smem(), vmem(), vmem()],
        out_specs=vmem(),
        compiler_params=params(52),
        cost_estimate=cost(0, 1 << 20),
        name="pack_third",
    )(codes, got1, got2)
    sent3, got2 = hold((sent3, got2))
    got3 = exchange(sent3, "req")
    held = lambda i: jnp.minimum(i, 7)
    part, fresh = pl.pallas_call(
        early_rows,
        out_shape=[packed((256, 2304), F32), packed((2048, 128), F32)],
        grid=(9,),
        in_specs=[
            pl.BlockSpec((16, 256), lambda i: (0, held(i))), whole(16, 2, 128),
            pl.BlockSpec((4, 256), lambda i: (0, held(i))), whole(4, 2, 128),
            pl.BlockSpec((64, 8, 128), lambda i: (0, 3, 0)),
            whole(1, 32), whole(256, 128), whole(256, 128), whole(32, 256), whole(256, 128), whole(32, 256),
            pl.BlockSpec((256, 256), lambda i: (0, held(i))), pl.BlockSpec((256, 128), lambda i: (held(i), 0)),
        ],
        out_specs=[cols(256, 256), pl.BlockSpec((256, 128), lambda i: (held(i), 0))],
        scratch_shapes=[
            pltpu.VMEM((16, 256), F32), pltpu.VMEM((16, 256), F32),
            pltpu.VMEM((256, 128), F32), pltpu.VMEM((128, 128), BF16), pltpu.VMEM((256, 128), BF16),
        ],
        compiler_params=params(52),
        cost_estimate=cost(1 << 29, 8 << 20),
        name="early_rows",
    )(
        inner_input, scan_args[1], inner_conv_taps, scan_args[3], got2, scan_args[7], c_main,
        decay, decay_t, step, step_t, part, fresh,
    )
    got3, part, fresh = hold((got3, part, fresh))

    normed, low = pl.pallas_call(
        state_kernel,
        out_shape=[packed((256, 2048), BF16), packed((8, 128, 128), BF16)],
        grid=(1,),
        in_specs=[whole(64, 32, 128), far, far, whole(1, 2048), whole(64, 56, 128)],
        out_specs=[far, far],
        scratch_shapes=[pltpu.VMEM((256, 2048), F32)] * 3
        + [pltpu.VMEM((128, 128), BF16), pltpu.VMEM((256, 128), F32), pltpu.VMEM((256, 2048), BF16), pltpu.SemaphoreType.DMA((2, 9))],
        compiler_params=params(52),
        cost_estimate=cost(1 << 28, 8 << 20),
        name="state",
    )(got3, part, gate, group_norm_gain.reshape(1, 2048), got2)
    low, fresh = hold((low, fresh))
    parts = exchange(low, "head")
    updated = pl.pallas_call(
        update_kernel,
        out_shape=packed((1, 2048, 128), BF16),
        in_specs=[vmem()] * 3,
        out_specs=vmem(),
        compiler_params=params(60),
        cost_estimate=cost(1 << 20, 3 << 20),
        name="update",
    )(got3, fresh, kept)
    parts, updated = hold((parts, updated))
    term = pl.pallas_call(
        up_kernel,
        out_shape=packed((256, 1024), BF16),
        in_specs=[vmem()] * 2,
        out_specs=vmem(),
        compiler_params=params(),
        cost_estimate=cost(1 << 26, 1 << 20),
        name="up",
    )(parts, got2)
    return normed, term, updated.reshape(1, 32, 64, 128)


def solution(mesh):
    return jax.shard_map(
        per_device,
        mesh=mesh,
        in_specs=(
            P("req", "head"),
            P("req", "head", None, None),
            P("req", "head"),
            P(None, "head"),
            P(None, "head", None, None),
            P("head"),
            P("head"),
            P("head"),
            P("head"),
            P("req"),
            P(),
            P("req"),
            P("req"),
            P("req", "head", None),
            P("req", None, "head"),
            P("req", "head", None, None),
            P("req", None, "head"),
            P("req", None, "head", None, None),
        ),
        out_specs=(P("req", "head"), P("req", "head"), P("req", "head", None, None)),
        check_vma=False,
    )
```

```python
import functools

import jax
import jax.numpy as jnp
from jax import lax
from jax.experimental import pallas as pl
from jax.experimental.pallas import tpu as pltpu
from jax.sharding import PartitionSpec as P

ADAPTER_SCALE = 2.0
NORM_EPSILON = 1e-05
F32, BF16 = jnp.float32, jnp.bfloat16
MIB = 1024 * 1024


def params(mib=20):
    return pltpu.CompilerParams(vmem_limit_bytes=mib * MIB)


def cost(flops, nbytes):
    return pl.CostEstimate(flops=flops, bytes_accessed=nbytes, transcendentals=0)


def smem():
    return pl.BlockSpec(memory_space=pltpu.SMEM)


def vmem():
    return pl.BlockSpec(memory_space=pltpu.VMEM)


def pack_first(tenant, table, owner, slot, down, up, convx, convbc, states, out):
    for chunk in range(64):
        col, row = chunk // 4, chunk % 4
        out[chunk, 0:16, :] = down[row * 16 : row * 16 + 16, col * 128 : col * 128 + 128]
        col, row = chunk // 8, chunk % 8
        out[chunk, 16:24, :] = up[0, row * 8 : row * 8 + 8, col * 128 : col * 128 + 128]
    lines = lax.broadcasted_iota(jnp.int32, (8, 128), 0)
    lanes = lax.broadcasted_iota(jnp.int32, (8, 128), 1)
    adapter = table[tenant[0]].astype(F32)
    base = jnp.where(lanes == 0, adapter, jnp.where(lanes == 1, owner[0].astype(F32), slot[0].astype(F32)))
    for chunk in range(64):
        tile = base
        if chunk < 54:
            for which in range(2):
                if chunk < 48:
                    k, col = chunk // 16, chunk % 16
                    line = convx[k, which : which + 1, col * 128 : col * 128 + 128]
                else:
                    k, side = (chunk - 48) // 2, (chunk - 48) % 2
                    line = convbc[which, k, 0, side : side + 1, :]
                tile = jnp.where(lines == which, jnp.broadcast_to(line.astype(F32), (8, 128)), tile)
        tile = jnp.where(lines >= 4, pltpu.roll(states[0, chunk].astype(F32), 6, 0), tile)
        tile = jnp.where(lines >= 6, states[1, chunk].astype(F32), tile)
        out[chunk, 24:32, :] = tile.astype(BF16)


def pack_second(me, first, states, out, codes, words, both, sems):
    fetches = [pltpu.make_async_copy(states.at[slot], both.at[slot], sems.at[1 + slot]) for slot in range(2)]
    for fetch in fetches:
        fetch.start()
    lines = lax.broadcasted_iota(jnp.int32, (8, 128), 0)
    tall = lax.broadcasted_iota(jnp.int32, (64, 8, 128), 1)
    picked = jnp.sum(jnp.where(tall == 2, first[:, 24:32, :].astype(F32), 0.0), axis=1)
    turned = jnp.concatenate([picked, jnp.zeros((64, 128), F32)], axis=0).T
    words[...] = turned[0:8, :].astype(jnp.int32)
    to_scalars = pltpu.make_async_copy(words, codes, sems.at[0])
    to_scalars.start()
    to_scalars.wait()
    mine = lax.fori_loop(0, 64, lambda j, m: jnp.where(codes[1, j] == me[0], codes[2, j], m), 0, unroll=8)
    for fetch in fetches:
        fetch.wait()

    def body(j, carry):
        out[j, 0:24, :] = both[mine, j, 0:24, :]
        out[j, 32:56, :] = first[codes[0, j], 0:24, :]
        tile = first[codes[1, j], 24:32, :].astype(F32)
        line = jnp.where(codes[2, j] == 0, tile[0:1], tile[1:2])
        out[j, 24:32, :] = jnp.where(lines == 6, line, both[mine, j, 24:32, :].astype(F32)).astype(BF16)
        return carry

    lax.fori_loop(0, 64, body, 0, unroll=8)


def pack_third(codes, first, second, out):
    lines = lax.broadcasted_iota(jnp.int32, (8, 128), 0)

    def body(j, carry):
        owner = codes[1, j]
        out[j, 0:24, :] = second[owner, 0:24, :]
        rest = first[owner, 24:32, :].astype(F32)
        rest = jnp.where(codes[2, j] == 0, pltpu.roll(rest, 2, 0), rest)
        out[j, 24:32, :] = jnp.where(lines >= 6, rest, second[owner, 24:32, :].astype(F32)).astype(BF16)
        return carry

    lax.fori_loop(0, 64, body, 0, unroll=8)


def silu(v):
    return v / (1.0 + jnp.exp(-v))


def history(convs, index):
    lines = lax.broadcasted_iota(jnp.int32, (8, 128), 0)
    old = [convs[i].astype(F32)[6:7, :] for i in index]
    return jnp.where(lines == 5, old[0], jnp.where(lines == 6, old[1], old[2]))


def conv(pad, taps, count):
    out = taps[0:1, :] * pad[5 : 5 + count, :]
    for k in range(1, 4):
        out = out + taps[k : k + 1, :] * pad[5 + k : 5 + count + k, :]
    return silu(out)


def conv_pair(pad, bc, taps, count):
    sides = []
    for side in range(2):
        at = slice(side * 128, side * 128 + 128)
        pad[8 : 8 + count, at] = bc[0:count, side, :].astype(F32)
        out = taps[0, side : side + 1, :] * pad[5 : 5 + count, at]
        for k in range(1, 4):
            out = out + taps[k, side : side + 1, :] * pad[5 + k : 5 + count + k, at]
        sides.append(silu(out))
    return jnp.concatenate(sides, axis=1)


def widened(value, lo, hi):
    left = lax.broadcasted_iota(jnp.int32, (value.shape[0], 128), 1) < 64
    return jnp.where(left, value[:, lo : lo + 1], value[:, hi : hi + 1])


def wide_row(row):
    return jnp.concatenate([row, jnp.zeros((1, 96), F32)], axis=1)


def dots(a, b, left, right):
    return lax.dot_general(a, b, (((left,), (right,)), ((), ())), preferred_element_type=F32)


def scan_kernel(flag, x, bc, taps, bc_taps, raw, bias, rate, skip, *rest):
    outs, (pad, pad_bc, score) = rest[-13:-3], rest[-3:]
    old = rest[:-13]
    part, gate, fresh, kept, c_out, b_out, decay, decay_t, step, step_t = outs
    block = pl.program_id(0)
    active = flag[0] == 1

    if old:

        @pl.when(jnp.logical_and(jnp.logical_not(active), block == 0))
        def _():
            for source, target in zip(old, outs):
                target[...] = source[...]

    @pl.when(jnp.logical_and(active, block == 0))
    def _():
        v = jnp.concatenate([raw[...].astype(F32), jnp.zeros((96, 256), F32)], axis=0).T + wide_row(bias[...])
        size = jnp.maximum(v, 0.0) + jnp.log(1.0 + jnp.exp(-jnp.abs(v)))
        drop = -wide_row(rate[...]) * size
        rows = lax.broadcasted_iota(jnp.int32, (256, 256), 0)
        cols = lax.broadcasted_iota(jnp.int32, (256, 256), 1)
        lower = (rows >= cols).astype(F32).astype(BF16)
        high = drop.astype(BF16)
        spare = drop - high.astype(F32)
        middle = spare.astype(BF16)
        low = (spare - middle.astype(F32)).astype(BF16)
        total = jnp.dot(lower, low, preferred_element_type=F32)
        total = total + jnp.dot(lower, middle, preferred_element_type=F32)
        total = total + jnp.dot(lower, high, preferred_element_type=F32)
        decay[...] = total
        step[...] = size
        decay_t[...] = total.T[0:32, :]
        step_t[...] = size.T[0:32, :]
        pad_bc[0:8, :] = jnp.zeros((8, 256), F32)
        both = jnp.where(rows >= 3, conv_pair(pad_bc, bc, bc_taps, 256), 0.0).astype(BF16)
        b_out[...] = both[:, 0:128]
        c_out[...] = both[:, 128:256]
        score[...] = dots(both[:, 128:256], both[:, 0:128], 1, 1)

    @pl.when(active)
    def _():
        pad[0:8, :] = jnp.zeros((8, 256), F32)
        pad[8:264, :] = x[...].astype(F32)
        tall = lax.broadcasted_iota(jnp.int32, (256, 256), 0)
        inner = jnp.where(tall >= 3, conv(pad, taps, 256), 0.0).astype(BF16)
        total = decay[...]
        shift = lax.rem(128 - 4 * block, 128)
        moved = pltpu.roll(total, shift, 1)
        grow = jnp.exp(moved)
        keep = pltpu.roll(jnp.exp(total[255:256, :] - total) * step[...], shift, 1)
        gains = pltpu.roll(jnp.broadcast_to(wide_row(skip[...]), (8, 128)), shift, 1)
        rows = lax.broadcasted_iota(jnp.int32, (128, 128), 0)
        cols = lax.broadcasted_iota(jnp.int32, (128, 128), 1)
        causal = rows >= cols
        left = cols < 64
        wide = inner.astype(F32)
        for pair in range(2):
            lo, hi = 2 * pair, 2 * pair + 1
            at = slice(pair * 128, pair * 128 + 128)
            values = inner[:, at]
            top, bottom = [], []
            for head in (lo, hi):
                here = moved[:, head : head + 1]
                there = decay_t[pl.ds(4 * block + head, 1), :]
                weight = step_t[pl.ds(4 * block + head, 1), :]
                gap = here[0:128] - there[:, 0:128]
                mix = score[0:128, 0:128] * jnp.exp(jnp.where(causal, gap, -jnp.inf)) * weight[:, 0:128]
                top.append(jnp.dot(mix.astype(BF16), values[0:128], preferred_element_type=F32))
                gap = here[128:256] - there[:, 0:128]
                mix = score[128:256, 0:128] * jnp.exp(gap) * weight[:, 0:128]
                early = mix.astype(BF16)
                gap = here[128:256] - there[:, 128:256]
                mix = score[128:256, 128:256] * jnp.exp(jnp.where(causal, gap, -jnp.inf)) * weight[:, 128:256]
                both = jnp.concatenate([early, mix.astype(BF16)], axis=1)
                bottom.append(jnp.dot(both, values, preferred_element_type=F32))
            gain = widened(gains[0:1, :], lo, hi)
            part[0:128, at] = jnp.where(left, top[0], top[1]) + gain * wide[0:128, at]
            part[128:256, at] = jnp.where(left, bottom[0], bottom[1]) + gain * wide[128:256, at]
            gate[:, at] = widened(grow, lo, hi)
            carried = (wide[:, at] * widened(keep, lo, hi)).astype(BF16)
            fresh[at, :] = dots(carried, b_out[...], 0, 0)
        for head in range(4):
            kept[head * 64 : head * 64 + 64, :] = jnp.broadcast_to(grow[255:256, head : head + 1], (64, 128))


def scan_first_kernel(flag, *refs):
    pack_refs, scan_refs, sent, scratch = refs[:9], refs[9:27], refs[27], refs[28:]

    @pl.when(pl.program_id(0) == 0)
    def _():
        pack_first(*pack_refs, sent)

    scan_kernel(flag, *scan_refs, *scratch)


def early_rows(
    x, bc, taps, bc_taps, convs, skip, c_main, decay, decay_t, step, step_t, part_in, fresh_in,
    part, fresh, pad, pad_bc, score, b_proj, c_all,
):
    block = pl.program_id(0)

    @pl.when(block == 8)
    def _():
        part[:, 0:128] = c_all[...].astype(F32)

    @pl.when(block < 8)
    def _():
        early_block(
            block, x, bc, taps, bc_taps, convs, skip, c_main, decay, decay_t, step, step_t, part_in, fresh_in,
            part, fresh, pad, pad_bc, score, b_proj, c_all,
        )


def early_block(
    block, x, bc, taps, bc_taps, convs, skip, c_main, decay, decay_t, step, step_t, part_in, fresh_in,
    part, fresh, pad, pad_bc, score, b_proj, c_proj,
):
    short = lax.broadcasted_iota(jnp.int32, (8, 256), 0) < 3
    rest = jnp.zeros((120, 128), F32)

    @pl.when(block == 0)
    def _():
        for side in range(2):
            at = slice(side * 128, side * 128 + 128)
            pad_bc[0:8, at] = history(convs, [48 + side, 50 + side, 52 + side])
        both = jnp.where(short, conv_pair(pad_bc, bc, bc_taps, 8), 0.0)
        b_proj[...] = jnp.concatenate([both[:, 0:128], rest], axis=0).astype(BF16)
        c_all = c_main[...].astype(F32)
        c_all = jnp.concatenate([c_all[0:8] + both[:, 128:256], c_all[8:256]], axis=0).astype(BF16)
        c_proj[...] = c_all
        score[...] = dots(c_all, b_proj[...], 1, 1)

    for half in range(2):
        at = slice(half * 128, half * 128 + 128)
        col = block * 2 + half
        pad[0:8, at] = history(convs, [col, col + 16, col + 32])
    pad[8:16, :] = x[0:8, :].astype(F32)
    inner = jnp.where(short, conv(pad, taps, 8), 0.0).astype(BF16).astype(F32)
    total = decay[...]
    shift = lax.rem(128 - 4 * block, 128)
    moved = pltpu.roll(total, shift, 1)
    keep = pltpu.roll(jnp.exp(total[255:256, :] - total[0:8, :]) * step[0:8, :], shift, 1)
    gains = pltpu.roll(jnp.broadcast_to(wide_row(skip[...]), (8, 128)), shift, 1)
    rows = lax.broadcasted_iota(jnp.int32, (256, 128), 0)
    cols = lax.broadcasted_iota(jnp.int32, (256, 128), 1)
    causal = rows >= cols
    left = cols < 64
    for pair in range(2):
        lo, hi = 2 * pair, 2 * pair + 1
        at = slice(pair * 128, pair * 128 + 128)
        values = jnp.concatenate([inner[:, at], rest], axis=0).astype(BF16)
        added = []
        for head in (lo, hi):
            gap = moved[:, head : head + 1] - decay_t[pl.ds(4 * block + head, 1), :][:, 0:128]
            weight = step_t[pl.ds(4 * block + head, 1), :][:, 0:128]
            mix = score[...] * jnp.exp(jnp.where(causal, gap, -jnp.inf)) * weight
            added.append(jnp.dot(mix.astype(BF16), values, preferred_element_type=F32))
        part[:, at] = part_in[:, at] + jnp.where(left, added[0], added[1])
        part[0:8, at] = part[0:8, at] + widened(gains[0:1, :], lo, hi) * inner[:, at]
        carried = (inner[:, at] * widened(keep, lo, hi)).astype(BF16).astype(F32)
        carried = jnp.concatenate([carried, rest], axis=0).astype(BF16)
        fresh[at, :] = fresh_in[at, :] + dots(carried, b_proj[...], 0, 0)


def state_kernel(state, part_far, gate_far, gain, panels, normed_far, low, mixed, part, gate, tile, c_proj, normed, sems):
    fetch = pltpu.make_async_copy(part_far.at[:, pl.ds(2048, 128)], c_proj, sems.at[0, 8])
    fetch.start()
    copies = []
    for block in range(8):
        at = pl.ds(block * 256, 256)
        copies.append(pltpu.make_async_copy(part_far.at[:, at], part.at[:, at], sems.at[0, block]))
        copies.append(pltpu.make_async_copy(gate_far.at[:, at], gate.at[:, at], sems.at[1, block]))
    for copy in copies:
        copy.start()
    fetch.wait()
    c_value = c_proj[...].astype(BF16)
    square = jnp.zeros((256, 128), F32)
    for block in range(8):
        at = slice(block * 256, block * 256 + 256)
        old = state[block * 8 : block * 8 + 8].reshape(256, 128)
        inter = lax.dot_general(c_value, old, (((1,), (1,)), ((), ())), preferred_element_type=F32)
        copies[2 * block].wait()
        copies[2 * block + 1].wait()
        total = part[:, at] + inter * gate[:, at]
        mixed[:, at] = total
        square = square + total[:, 0:128] * total[:, 0:128] + total[:, 128:256] * total[:, 128:256]
    mean = jnp.sum(square, axis=1, keepdims=True) * (1.0 / 2048.0)
    scale = lax.rsqrt(mean + NORM_EPSILON)
    acc = jnp.zeros((256, 64), F32)
    leaving = []
    for col in range(16):
        at = slice(col * 128, col * 128 + 128)
        value = (mixed[:, at] * scale * gain[:, at]).astype(BF16)
        normed[:, at] = value
        panel = panels[col * 4 : col * 4 + 4, 32:48, :].reshape(64, 128)
        acc = acc + lax.dot_general(value, panel, (((1,), (1,)), ((), ())), preferred_element_type=F32)
        if col % 4 == 3:
            at = pl.ds(col * 128 - 384, 512)
            leaving.append(pltpu.make_async_copy(normed.at[:, at], normed_far.at[:, at], sems.at[1, col // 4]))
            leaving[-1].start()
    tile[...] = jnp.concatenate([acc[0:128], acc[128:256]], axis=1).astype(BF16)
    copies = [pltpu.make_async_copy(tile, low.at[peer], sems.at[0, peer]) for peer in range(8)]
    for copy in copies:
        copy.start()
    for copy in copies + leaving:
        copy.wait()


def update_kernel(state, fresh, kept, updated):
    updated[0] = (fresh[...] + kept[...] * state[...].reshape(2048, 128).astype(F32)).astype(BF16)


def up_kernel(parts, up, out):
    total = parts[0].astype(F32)
    for peer in range(1, 8):
        total = total + parts[peer].astype(F32)
    reduced = total.astype(BF16)
    halves = [reduced[:, 0:64], reduced[:, 64:128]]
    for col in range(8):
        panel = up[col * 8 : col * 8 + 8, 48:56, :].astype(F32).reshape(64, 128).astype(BF16)
        at = slice(col * 128, col * 128 + 128)
        for half in range(2):
            value = jnp.dot(halves[half], panel, preferred_element_type=F32) * ADAPTER_SCALE
            out[half * 128 : half * 128 + 128, at] = value.astype(BF16)


def exchange(value, axis):
    return lax.all_to_all(value, axis, split_axis=0, concat_axis=0, tiled=True)


def per_device(
    inner_input,
    projection_input,
    step_before_bias,
    inner_conv_taps,
    projection_conv_taps,
    step_bias,
    head_decay_rate,
    head_skip_gain,
    group_norm_gain,
    tenant,
    tenant_adapter_row,
    cache_holder_index,
    cache_slot_index,
    adapter_down_panels,
    adapter_up_panels,
    cached_ssm_states,
    inner_conv_cache,
    projection_conv_cache,
):
    hold = lax.optimization_barrier
    packed = jax.ShapeDtypeStruct
    whole = lambda *shape: pl.BlockSpec(shape, lambda i: (0,) * len(shape))
    far = pl.BlockSpec(memory_space=pltpu.HBM)
    states = cached_ssm_states.reshape(2, 64, 32, 128)
    pack_args = [
        tenant, tenant_adapter_row, cache_holder_index, cache_slot_index,
        jnp.swapaxes(adapter_down_panels, 1, 2).reshape(64, 2048), adapter_up_panels,
        jnp.swapaxes(inner_conv_cache, 0, 1), projection_conv_cache, states,
    ]
    even = 1 - (lax.axis_index("head").astype(jnp.int32) & 1)
    cols = lambda *shape: pl.BlockSpec(shape, lambda i: (0,) * (len(shape) - 1) + (i,))
    scan_shapes = [
        packed((256, 2048), F32), packed((256, 2048), F32), packed((2048, 128), F32), packed((2048, 128), F32),
        packed((256, 128), BF16), packed((256, 128), BF16), packed((256, 128), F32), packed((32, 256), F32),
        packed((256, 128), F32), packed((32, 256), F32),
    ]
    wide_at = lambda *shape: pl.BlockSpec(shape, lambda i, on: (0, i * on[0]))
    tall_at = lambda *shape: pl.BlockSpec(shape, lambda i, on: (i * on[0], 0))
    fixed = lambda *shape: pl.BlockSpec(shape, lambda i, on: (0,) * len(shape))
    scan_specs = [
        wide_at(256, 256), wide_at(256, 256), tall_at(256, 128), tall_at(256, 128),
        fixed(256, 128), fixed(256, 128), fixed(256, 128), fixed(32, 256), fixed(256, 128), fixed(32, 256),
    ]
    scan_args = [
        inner_input, projection_input.reshape(256, 2, 128), inner_conv_taps, projection_conv_taps.reshape(4, 2, 128),
        step_before_bias.T, step_bias.reshape(1, 32), head_decay_rate.reshape(1, 32), head_skip_gain.reshape(1, 32),
    ]

    sent1 = pl.pallas_call(
        pack_first,
        out_shape=packed((64, 32, 128), BF16),
        grid=(1,),
        in_specs=[smem()] * 4
        + [
            whole(64, 2048), whole(1, 64, 1024), whole(3, 2, 2048), whole(2, 3, 1, 2, 128),
            pl.BlockSpec((2, 64, 8, 128), lambda i: (0, 0, 3, 0)),
        ],
        out_specs=whole(64, 32, 128),
        compiler_params=params(60),
        cost_estimate=cost(0, 2 << 20),
        name="pack_first",
    )(*pack_args)

    def scan(on, old, limit):
        inputs = [
            wide_at(256, 256), fixed(256, 2, 128), wide_at(4, 256), fixed(4, 2, 128), fixed(32, 256),
            fixed(1, 32), fixed(1, 32), fixed(1, 32),
        ]
        first, pack_specs = False, []
        return pl.pallas_call(
            scan_first_kernel if first else scan_kernel,
            out_shape=scan_shapes + [packed((64, 32, 128), BF16)] * first,
            grid_spec=pltpu.PrefetchScalarGridSpec(
                num_scalar_prefetch=1,
                grid=(8,),
                in_specs=pack_specs * first + inputs + scan_specs[: len(old)],
                out_specs=scan_specs + [fixed(64, 32, 128)] * first,
                scratch_shapes=[pltpu.VMEM((264, 256), F32), pltpu.VMEM((264, 256), F32), pltpu.VMEM((256, 256), F32)],
            ),
            input_output_aliases={9 + i: i for i in range(len(old))},
            compiler_params=params(limit),
            cost_estimate=cost(2 << 30, 10 << 20),
            name="scan_late" if old else "scan_early",
        )(on.reshape(1), *(pack_args * first), *scan_args, *old)

    skipped = pl.pallas_call(
        lambda *refs: None, out_shape=scan_shapes, out_specs=[far] * 10, compiler_params=params(60), name="skip"
    )
    early = lax.cond(even == 1, lambda: scan(jnp.int32(1), [], 60), lambda: skipped())
    sent1, *early = hold((sent1, *early))
    got1 = exchange(sent1, "req")
    late = scan(1 - even, early, 60)
    me = lax.axis_index("req").astype(jnp.int32).reshape(1)
    got1, me, *late = hold((got1, me, *late))
    part, gate, fresh, kept, c_main, b_main, decay, decay_t, step, step_t = late

    sent2, codes = pl.pallas_call(
        pack_second,
        out_shape=[packed((64, 56, 128), BF16), packed((8, 128), jnp.int32)],
        in_specs=[smem(), vmem(), pl.BlockSpec(memory_space=pl.ANY)],
        out_specs=[vmem(), smem()],
        scratch_shapes=[
            pltpu.VMEM((8, 128), jnp.int32), pltpu.VMEM((2, 64, 32, 128), BF16), pltpu.SemaphoreType.DMA((3,)),
        ],
        compiler_params=params(52),
        cost_estimate=cost(0, 3 << 20),
        name="pack_second",
    )(me, got1, states)
    got2 = exchange(sent2, "req")
    sent3 = pl.pallas_call(
        pack_third,
        out_shape=packed((64, 32, 128), BF16),
        in_specs=[smem(), vmem(), vmem()],
        out_specs=vmem(),
        compiler_params=params(52),
        cost_estimate=cost(0, 1 << 20),
        name="pack_third",
    )(codes, got1, got2)
    sent3, got2 = hold((sent3, got2))
    got3 = exchange(sent3, "req")
    held = lambda i: jnp.minimum(i, 7)
    part, fresh = pl.pallas_call(
        early_rows,
        out_shape=[packed((256, 2304), F32), packed((2048, 128), F32)],
        grid=(9,),
        in_specs=[
            pl.BlockSpec((16, 256), lambda i: (0, held(i))), whole(16, 2, 128),
            pl.BlockSpec((4, 256), lambda i: (0, held(i))), whole(4, 2, 128),
            pl.BlockSpec((64, 8, 128), lambda i: (0, 3, 0)),
            whole(1, 32), whole(256, 128), whole(256, 128), whole(32, 256), whole(256, 128), whole(32, 256),
            pl.BlockSpec((256, 256), lambda i: (0, held(i))), pl.BlockSpec((256, 128), lambda i: (held(i), 0)),
        ],
        out_specs=[cols(256, 256), pl.BlockSpec((256, 128), lambda i: (held(i), 0))],
        scratch_shapes=[
            pltpu.VMEM((16, 256), F32), pltpu.VMEM((16, 256), F32),
            pltpu.VMEM((256, 128), F32), pltpu.VMEM((128, 128), BF16), pltpu.VMEM((256, 128), BF16),
        ],
        compiler_params=params(52),
        cost_estimate=cost(1 << 29, 8 << 20),
        name="early_rows",
    )(
        inner_input, scan_args[1], inner_conv_taps, scan_args[3], got2, scan_args[7], c_main,
        decay, decay_t, step, step_t, part, fresh,
    )
    got3, part, fresh = hold((got3, part, fresh))

    normed, low = pl.pallas_call(
        state_kernel,
        out_shape=[packed((256, 2048), BF16), packed((8, 128, 128), BF16)],
        in_specs=[vmem(), far, far, vmem(), vmem()],
        out_specs=[far, far],
        scratch_shapes=[pltpu.VMEM((256, 2048), F32)] * 3
        + [pltpu.VMEM((128, 128), BF16), pltpu.VMEM((256, 128), F32), pltpu.VMEM((256, 2048), BF16), pltpu.SemaphoreType.DMA((2, 9))],
        compiler_params=params(52),
        cost_estimate=cost(1 << 28, 8 << 20),
        name="state",
    )(got3, part, gate, group_norm_gain.reshape(1, 2048), got2)
    low, fresh = hold((low, fresh))
    parts = exchange(low, "head")
    updated = pl.pallas_call(
        update_kernel,
        out_shape=packed((1, 2048, 128), BF16),
        in_specs=[vmem()] * 3,
        out_specs=vmem(),
        compiler_params=params(60),
        cost_estimate=cost(1 << 20, 3 << 20),
        name="update",
    )(got3, fresh, kept)
    parts, updated = hold((parts, updated))
    term = pl.pallas_call(
        up_kernel,
        out_shape=packed((256, 1024), BF16),
        in_specs=[vmem()] * 2,
        out_specs=vmem(),
        compiler_params=params(),
        cost_estimate=cost(1 << 26, 1 << 20),
        name="up",
    )(parts, got2)
    return normed, term, updated.reshape(1, 32, 64, 128)


def solution(mesh):
    return jax.shard_map(
        per_device,
        mesh=mesh,
        in_specs=(
            P("req", "head"),
            P("req", "head", None, None),
            P("req", "head"),
            P(None, "head"),
            P(None, "head", None, None),
            P("head"),
            P("head"),
            P("head"),
            P("head"),
            P("req"),
            P(),
            P("req"),
            P("req"),
            P("req", "head", None),
            P("req", None, "head"),
            P("req", "head", None, None),
            P("req", None, "head"),
            P("req", None, "head", None, None),
        ),
        out_specs=(P("req", "head"), P("req", "head"), P("req", "head", None, None)),
        check_vma=False,
    )
```

```python
import functools

import jax
import jax.numpy as jnp
from jax import lax
from jax.experimental import pallas as pl
from jax.experimental.pallas import tpu as pltpu
from jax.sharding import PartitionSpec as P

ADAPTER_SCALE = 2.0
NORM_EPSILON = 1e-05
F32, BF16 = jnp.float32, jnp.bfloat16
MIB = 1024 * 1024


def params(mib=20):
    return pltpu.CompilerParams(vmem_limit_bytes=mib * MIB)


def cost(flops, nbytes):
    return pl.CostEstimate(flops=flops, bytes_accessed=nbytes, transcendentals=0)


def smem():
    return pl.BlockSpec(memory_space=pltpu.SMEM)


def vmem():
    return pl.BlockSpec(memory_space=pltpu.VMEM)


def pack_first(tenant, table, owner, slot, down, up, convx, convbc, states, out):
    for chunk in range(64):
        col, row = chunk // 4, chunk % 4
        out[chunk, 0:16, :] = down[row * 16 : row * 16 + 16, col * 128 : col * 128 + 128]
        col, row = chunk // 8, chunk % 8
        out[chunk, 16:24, :] = up[0, row * 8 : row * 8 + 8, col * 128 : col * 128 + 128]
    lines = lax.broadcasted_iota(jnp.int32, (8, 128), 0)
    lanes = lax.broadcasted_iota(jnp.int32, (8, 128), 1)
    adapter = table[tenant[0]].astype(F32)
    base = jnp.where(lanes == 0, adapter, jnp.where(lanes == 1, owner[0].astype(F32), slot[0].astype(F32)))
    for chunk in range(64):
        tile = base
        if chunk < 54:
            for which in range(2):
                if chunk < 48:
                    k, col = chunk // 16, chunk % 16
                    line = convx[k, which : which + 1, col * 128 : col * 128 + 128]
                else:
                    k, side = (chunk - 48) // 2, (chunk - 48) % 2
                    line = convbc[which, k, 0, side : side + 1, :]
                tile = jnp.where(lines == which, jnp.broadcast_to(line.astype(F32), (8, 128)), tile)
        tile = jnp.where(lines >= 4, pltpu.roll(states[0, chunk].astype(F32), 6, 0), tile)
        tile = jnp.where(lines >= 6, states[1, chunk].astype(F32), tile)
        out[chunk, 24:32, :] = tile.astype(BF16)


def pack_second(me, first, states, out, codes, words, both, sems):
    fetches = [pltpu.make_async_copy(states.at[slot], both.at[slot], sems.at[1 + slot]) for slot in range(2)]
    for fetch in fetches:
        fetch.start()
    lines = lax.broadcasted_iota(jnp.int32, (8, 128), 0)
    tall = lax.broadcasted_iota(jnp.int32, (64, 8, 128), 1)
    picked = jnp.sum(jnp.where(tall == 2, first[:, 24:32, :].astype(F32), 0.0), axis=1)
    turned = jnp.concatenate([picked, jnp.zeros((64, 128), F32)], axis=0).T
    words[...] = turned[0:8, :].astype(jnp.int32)
    to_scalars = pltpu.make_async_copy(words, codes, sems.at[0])
    to_scalars.start()
    to_scalars.wait()
    mine = lax.fori_loop(0, 64, lambda j, m: jnp.where(codes[1, j] == me[0], codes[2, j], m), 0, unroll=8)
    for fetch in fetches:
        fetch.wait()

    def body(j, carry):
        out[j, 0:24, :] = both[mine, j, 0:24, :]
        out[j, 32:48, :] = first[codes[0, j], 0:16, :]
        tile = first[codes[1, j], 24:32, :].astype(F32)
        line = jnp.where(codes[2, j] == 0, tile[0:1], tile[1:2])
        out[j, 24:32, :] = jnp.where(lines == 6, line, both[mine, j, 24:32, :].astype(F32)).astype(BF16)
        return carry

    lax.fori_loop(0, 64, body, 0, unroll=8)


def pack_third(codes, first, second, out):
    lines = lax.broadcasted_iota(jnp.int32, (8, 128), 0)

    def body(j, carry):
        owner = codes[1, j]
        out[j, 0:24, :] = second[owner, 0:24, :]
        out[j, 32:40, :] = first[codes[0, j], 16:24, :]
        rest = first[owner, 24:32, :].astype(F32)
        rest = jnp.where(codes[2, j] == 0, pltpu.roll(rest, 2, 0), rest)
        out[j, 24:32, :] = jnp.where(lines >= 6, rest, second[owner, 24:32, :].astype(F32)).astype(BF16)
        return carry

    lax.fori_loop(0, 64, body, 0, unroll=8)


def silu(v):
    return v / (1.0 + jnp.exp(-v))


def history(convs, index):
    lines = lax.broadcasted_iota(jnp.int32, (8, 128), 0)
    old = [convs[i].astype(F32)[6:7, :] for i in index]
    return jnp.where(lines == 5, old[0], jnp.where(lines == 6, old[1], old[2]))


def conv(pad, taps, count):
    out = taps[0:1, :] * pad[5 : 5 + count, :]
    for k in range(1, 4):
        out = out + taps[k : k + 1, :] * pad[5 + k : 5 + count + k, :]
    return silu(out)


def conv_pair(pad, bc, taps, count):
    sides = []
    for side in range(2):
        at = slice(side * 128, side * 128 + 128)
        pad[8 : 8 + count, at] = bc[0:count, side, :].astype(F32)
        out = taps[0, side : side + 1, :] * pad[5 : 5 + count, at]
        for k in range(1, 4):
            out = out + taps[k, side : side + 1, :] * pad[5 + k : 5 + count + k, at]
        sides.append(silu(out))
    return jnp.concatenate(sides, axis=1)


def widened(value, lo, hi):
    left = lax.broadcasted_iota(jnp.int32, (value.shape[0], 128), 1) < 64
    return jnp.where(left, value[:, lo : lo + 1], value[:, hi : hi + 1])


def wide_row(row):
    return jnp.concatenate([row, jnp.zeros((1, 96), F32)], axis=1)


def dots(a, b, left, right):
    return lax.dot_general(a, b, (((left,), (right,)), ((), ())), preferred_element_type=F32)


def scan_kernel(flag, x, bc, taps, bc_taps, raw, bias, rate, skip, *rest):
    outs, (pad, pad_bc, score) = rest[-13:-3], rest[-3:]
    old = rest[:-13]
    part, gate, fresh, kept, c_out, b_out, decay, decay_t, step, step_t = outs
    block = pl.program_id(0)
    active = flag[0] == 1

    if old:

        @pl.when(jnp.logical_and(jnp.logical_not(active), block == 0))
        def _():
            for source, target in zip(old, outs):
                target[...] = source[...]

    @pl.when(jnp.logical_and(active, block == 0))
    def _():
        v = jnp.concatenate([raw[...].astype(F32), jnp.zeros((96, 256), F32)], axis=0).T + wide_row(bias[...])
        size = jnp.maximum(v, 0.0) + jnp.log(1.0 + jnp.exp(-jnp.abs(v)))
        drop = -wide_row(rate[...]) * size
        rows = lax.broadcasted_iota(jnp.int32, (256, 256), 0)
        cols = lax.broadcasted_iota(jnp.int32, (256, 256), 1)
        lower = (rows >= cols).astype(F32).astype(BF16)
        high = drop.astype(BF16)
        spare = drop - high.astype(F32)
        middle = spare.astype(BF16)
        low = (spare - middle.astype(F32)).astype(BF16)
        total = jnp.dot(lower, low, preferred_element_type=F32)
        total = total + jnp.dot(lower, middle, preferred_element_type=F32)
        total = total + jnp.dot(lower, high, preferred_element_type=F32)
        decay[...] = total
        step[...] = size
        decay_t[...] = total.T[0:32, :]
        step_t[...] = size.T[0:32, :]
        pad_bc[0:8, :] = jnp.zeros((8, 256), F32)
        both = jnp.where(rows >= 3, conv_pair(pad_bc, bc, bc_taps, 256), 0.0).astype(BF16)
        b_out[...] = both[:, 0:128]
        c_out[...] = both[:, 128:256]
        score[...] = dots(both[:, 128:256], both[:, 0:128], 1, 1)

    @pl.when(active)
    def _():
        pad[0:8, :] = jnp.zeros((8, 256), F32)
        pad[8:264, :] = x[...].astype(F32)
        tall = lax.broadcasted_iota(jnp.int32, (256, 256), 0)
        inner = jnp.where(tall >= 3, conv(pad, taps, 256), 0.0).astype(BF16)
        total = decay[...]
        shift = lax.rem(128 - 4 * block, 128)
        moved = pltpu.roll(total, shift, 1)
        grow = jnp.exp(moved)
        keep = pltpu.roll(jnp.exp(total[255:256, :] - total) * step[...], shift, 1)
        gains = pltpu.roll(jnp.broadcast_to(wide_row(skip[...]), (8, 128)), shift, 1)
        rows = lax.broadcasted_iota(jnp.int32, (128, 128), 0)
        cols = lax.broadcasted_iota(jnp.int32, (128, 128), 1)
        causal = rows >= cols
        left = cols < 64
        wide = inner.astype(F32)
        for pair in range(2):
            lo, hi = 2 * pair, 2 * pair + 1
            at = slice(pair * 128, pair * 128 + 128)
            values = inner[:, at]
            top, bottom = [], []
            for head in (lo, hi):
                here = moved[:, head : head + 1]
                there = decay_t[pl.ds(4 * block + head, 1), :]
                weight = step_t[pl.ds(4 * block + head, 1), :]
                gap = here[0:128] - there[:, 0:128]
                mix = score[0:128, 0:128] * jnp.exp(jnp.where(causal, gap, -jnp.inf)) * weight[:, 0:128]
                top.append(jnp.dot(mix.astype(BF16), values[0:128], preferred_element_type=F32))
                gap = here[128:256] - there[:, 0:128]
                mix = score[128:256, 0:128] * jnp.exp(gap) * weight[:, 0:128]
                early = mix.astype(BF16)
                gap = here[128:256] - there[:, 128:256]
                mix = score[128:256, 128:256] * jnp.exp(jnp.where(causal, gap, -jnp.inf)) * weight[:, 128:256]
                both = jnp.concatenate([early, mix.astype(BF16)], axis=1)
                bottom.append(jnp.dot(both, values, preferred_element_type=F32))
            gain = widened(gains[0:1, :], lo, hi)
            part[0:128, at] = jnp.where(left, top[0], top[1]) + gain * wide[0:128, at]
            part[128:256, at] = jnp.where(left, bottom[0], bottom[1]) + gain * wide[128:256, at]
            gate[:, at] = widened(grow, lo, hi)
            carried = (wide[:, at] * widened(keep, lo, hi)).astype(BF16)
            fresh[at, :] = dots(carried, b_out[...], 0, 0)
        for head in range(4):
            kept[head * 64 : head * 64 + 64, :] = jnp.broadcast_to(grow[255:256, head : head + 1], (64, 128))


def scan_first_kernel(flag, *refs):
    pack_refs, scan_refs, sent, scratch = refs[:9], refs[9:27], refs[27], refs[28:]

    @pl.when(pl.program_id(0) == 0)
    def _():
        pack_first(*pack_refs, sent)

    scan_kernel(flag, *scan_refs, *scratch)


def early_rows(
    x, bc, taps, bc_taps, convs, skip, c_main, decay, decay_t, step, step_t, part_in, fresh_in,
    part, fresh, pad, pad_bc, score, b_proj, c_all,
):
    block = pl.program_id(0)

    @pl.when(block == 8)
    def _():
        part[:, 0:128] = c_all[...].astype(F32)

    @pl.when(block < 8)
    def _():
        early_block(
            block, x, bc, taps, bc_taps, convs, skip, c_main, decay, decay_t, step, step_t, part_in, fresh_in,
            part, fresh, pad, pad_bc, score, b_proj, c_all,
        )


def early_block(
    block, x, bc, taps, bc_taps, convs, skip, c_main, decay, decay_t, step, step_t, part_in, fresh_in,
    part, fresh, pad, pad_bc, score, b_proj, c_proj,
):
    short = lax.broadcasted_iota(jnp.int32, (8, 256), 0) < 3
    rest = jnp.zeros((120, 128), F32)

    @pl.when(block == 0)
    def _():
        for side in range(2):
            at = slice(side * 128, side * 128 + 128)
            pad_bc[0:8, at] = history(convs, [48 + side, 50 + side, 52 + side])
        both = jnp.where(short, conv_pair(pad_bc, bc, bc_taps, 8), 0.0)
        b_proj[...] = jnp.concatenate([both[:, 0:128], rest], axis=0).astype(BF16)
        c_all = c_main[...].astype(F32)
        c_all = jnp.concatenate([c_all[0:8] + both[:, 128:256], c_all[8:256]], axis=0).astype(BF16)
        c_proj[...] = c_all
        score[...] = dots(c_all, b_proj[...], 1, 1)

    for half in range(2):
        at = slice(half * 128, half * 128 + 128)
        col = block * 2 + half
        pad[0:8, at] = history(convs, [col, col + 16, col + 32])
    pad[8:16, :] = x[0:8, :].astype(F32)
    inner = jnp.where(short, conv(pad, taps, 8), 0.0).astype(BF16).astype(F32)
    total = decay[...]
    shift = lax.rem(128 - 4 * block, 128)
    moved = pltpu.roll(total, shift, 1)
    keep = pltpu.roll(jnp.exp(total[255:256, :] - total[0:8, :]) * step[0:8, :], shift, 1)
    gains = pltpu.roll(jnp.broadcast_to(wide_row(skip[...]), (8, 128)), shift, 1)
    rows = lax.broadcasted_iota(jnp.int32, (256, 128), 0)
    cols = lax.broadcasted_iota(jnp.int32, (256, 128), 1)
    causal = rows >= cols
    left = cols < 64
    for pair in range(2):
        lo, hi = 2 * pair, 2 * pair + 1
        at = slice(pair * 128, pair * 128 + 128)
        values = jnp.concatenate([inner[:, at], rest], axis=0).astype(BF16)
        added = []
        for head in (lo, hi):
            gap = moved[:, head : head + 1] - decay_t[pl.ds(4 * block + head, 1), :][:, 0:128]
            weight = step_t[pl.ds(4 * block + head, 1), :][:, 0:128]
            mix = score[...] * jnp.exp(jnp.where(causal, gap, -jnp.inf)) * weight
            added.append(jnp.dot(mix.astype(BF16), values, preferred_element_type=F32))
        part[:, at] = part_in[:, at] + jnp.where(left, added[0], added[1])
        part[0:8, at] = part[0:8, at] + widened(gains[0:1, :], lo, hi) * inner[:, at]
        carried = (inner[:, at] * widened(keep, lo, hi)).astype(BF16).astype(F32)
        carried = jnp.concatenate([carried, rest], axis=0).astype(BF16)
        fresh[at, :] = fresh_in[at, :] + dots(carried, b_proj[...], 0, 0)


def state_kernel(state, part_far, gate_far, gain, panels, normed_far, low, mixed, part, gate, tile, c_proj, normed, sems):
    fetch = pltpu.make_async_copy(part_far.at[:, pl.ds(2048, 128)], c_proj, sems.at[0, 8])
    fetch.start()
    copies = []
    for block in range(8):
        at = pl.ds(block * 256, 256)
        copies.append(pltpu.make_async_copy(part_far.at[:, at], part.at[:, at], sems.at[0, block]))
        copies.append(pltpu.make_async_copy(gate_far.at[:, at], gate.at[:, at], sems.at[1, block]))
    for copy in copies:
        copy.start()
    fetch.wait()
    c_value = c_proj[...].astype(BF16)
    square = jnp.zeros((256, 128), F32)
    for block in range(8):
        at = slice(block * 256, block * 256 + 256)
        old = state[block * 8 : block * 8 + 8, 0:32, :].reshape(256, 128)
        inter = lax.dot_general(c_value, old, (((1,), (1,)), ((), ())), preferred_element_type=F32)
        copies[2 * block].wait()
        copies[2 * block + 1].wait()
        total = part[:, at] + inter * gate[:, at]
        mixed[:, at] = total
        square = square + total[:, 0:128] * total[:, 0:128] + total[:, 128:256] * total[:, 128:256]
    mean = jnp.sum(square, axis=1, keepdims=True) * (1.0 / 2048.0)
    scale = lax.rsqrt(mean + NORM_EPSILON)
    acc = jnp.zeros((256, 64), F32)
    leaving = []
    for col in range(16):
        at = slice(col * 128, col * 128 + 128)
        value = (mixed[:, at] * scale * gain[:, at]).astype(BF16)
        normed[:, at] = value
        panel = panels[col * 4 : col * 4 + 4, 32:48, :].reshape(64, 128)
        acc = acc + lax.dot_general(value, panel, (((1,), (1,)), ((), ())), preferred_element_type=F32)
        if col % 4 == 3:
            at = pl.ds(col * 128 - 384, 512)
            leaving.append(pltpu.make_async_copy(normed.at[:, at], normed_far.at[:, at], sems.at[1, col // 4]))
            leaving[-1].start()
    tile[...] = jnp.concatenate([acc[0:128], acc[128:256]], axis=1).astype(BF16)
    copies = [pltpu.make_async_copy(tile, low.at[peer], sems.at[0, peer]) for peer in range(8)]
    for copy in copies:
        copy.start()
    for copy in copies + leaving:
        copy.wait()


def update_kernel(state, fresh, kept, updated):
    updated[0] = (fresh[...] + kept[...] * state[:, 0:32, :].reshape(2048, 128).astype(F32)).astype(BF16)


def up_kernel(parts, up, out):
    total = parts[0].astype(F32)
    for peer in range(1, 8):
        total = total + parts[peer].astype(F32)
    reduced = total.astype(BF16)
    halves = [reduced[:, 0:64], reduced[:, 64:128]]
    for col in range(8):
        panel = up[col * 8 : col * 8 + 8, 32:40, :].astype(F32).reshape(64, 128).astype(BF16)
        at = slice(col * 128, col * 128 + 128)
        for half in range(2):
            value = jnp.dot(halves[half], panel, preferred_element_type=F32) * ADAPTER_SCALE
            out[half * 128 : half * 128 + 128, at] = value.astype(BF16)


def exchange(value, axis):
    return lax.all_to_all(value, axis, split_axis=0, concat_axis=0, tiled=True)


def per_device(
    inner_input,
    projection_input,
    step_before_bias,
    inner_conv_taps,
    projection_conv_taps,
    step_bias,
    head_decay_rate,
    head_skip_gain,
    group_norm_gain,
    tenant,
    tenant_adapter_row,
    cache_holder_index,
    cache_slot_index,
    adapter_down_panels,
    adapter_up_panels,
    cached_ssm_states,
    inner_conv_cache,
    projection_conv_cache,
):
    hold = lax.optimization_barrier
    packed = jax.ShapeDtypeStruct
    whole = lambda *shape: pl.BlockSpec(shape, lambda i: (0,) * len(shape))
    far = pl.BlockSpec(memory_space=pltpu.HBM)
    states = cached_ssm_states.reshape(2, 64, 32, 128)
    pack_args = [
        tenant, tenant_adapter_row, cache_holder_index, cache_slot_index,
        jnp.swapaxes(adapter_down_panels, 1, 2).reshape(64, 2048), adapter_up_panels,
        jnp.swapaxes(inner_conv_cache, 0, 1), projection_conv_cache, states,
    ]
    even = 1 - (lax.axis_index("head").astype(jnp.int32) & 1)
    cols = lambda *shape: pl.BlockSpec(shape, lambda i: (0,) * (len(shape) - 1) + (i,))
    scan_shapes = [
        packed((256, 2048), F32), packed((256, 2048), F32), packed((2048, 128), F32), packed((2048, 128), F32),
        packed((256, 128), BF16), packed((256, 128), BF16), packed((256, 128), F32), packed((32, 256), F32),
        packed((256, 128), F32), packed((32, 256), F32),
    ]
    wide_at = lambda *shape: pl.BlockSpec(shape, lambda i, on: (0, i * on[0]))
    tall_at = lambda *shape: pl.BlockSpec(shape, lambda i, on: (i * on[0], 0))
    fixed = lambda *shape: pl.BlockSpec(shape, lambda i, on: (0,) * len(shape))
    scan_specs = [
        wide_at(256, 256), wide_at(256, 256), tall_at(256, 128), tall_at(256, 128),
        fixed(256, 128), fixed(256, 128), fixed(256, 128), fixed(32, 256), fixed(256, 128), fixed(32, 256),
    ]
    scan_args = [
        inner_input, projection_input.reshape(256, 2, 128), inner_conv_taps, projection_conv_taps.reshape(4, 2, 128),
        step_before_bias.T, step_bias.reshape(1, 32), head_decay_rate.reshape(1, 32), head_skip_gain.reshape(1, 32),
    ]

    sent1 = pl.pallas_call(
        pack_first,
        out_shape=packed((64, 32, 128), BF16),
        grid=(1,),
        in_specs=[smem()] * 4
        + [
            whole(64, 2048), whole(1, 64, 1024), whole(3, 2, 2048), whole(2, 3, 1, 2, 128),
            pl.BlockSpec((2, 64, 8, 128), lambda i: (0, 0, 3, 0)),
        ],
        out_specs=whole(64, 32, 128),
        compiler_params=params(60),
        cost_estimate=cost(0, 2 << 20),
        name="pack_first",
    )(*pack_args)

    def scan(on, old, limit):
        inputs = [
            wide_at(256, 256), fixed(256, 2, 128), wide_at(4, 256), fixed(4, 2, 128), fixed(32, 256),
            fixed(1, 32), fixed(1, 32), fixed(1, 32),
        ]
        first, pack_specs = False, []
        return pl.pallas_call(
            scan_first_kernel if first else scan_kernel,
            out_shape=scan_shapes + [packed((64, 32, 128), BF16)] * first,
            grid_spec=pltpu.PrefetchScalarGridSpec(
                num_scalar_prefetch=1,
                grid=(8,),
                in_specs=pack_specs * first + inputs + scan_specs[: len(old)],
                out_specs=scan_specs + [fixed(64, 32, 128)] * first,
                scratch_shapes=[pltpu.VMEM((264, 256), F32), pltpu.VMEM((264, 256), F32), pltpu.VMEM((256, 256), F32)],
            ),
            input_output_aliases={9 + i: i for i in range(len(old))},
            compiler_params=params(limit),
            cost_estimate=cost(2 << 30, 10 << 20),
            name="scan_late" if old else "scan_early",
        )(on.reshape(1), *(pack_args * first), *scan_args, *old)

    skipped = pl.pallas_call(
        lambda *refs: None, out_shape=scan_shapes, out_specs=[far] * 10, compiler_params=params(60), name="skip"
    )
    early = lax.cond(even == 1, lambda: scan(jnp.int32(1), [], 60), lambda: skipped())
    sent1, *early = hold((sent1, *early))
    got1 = exchange(sent1, "req")
    late = scan(1 - even, early, 60)
    me = lax.axis_index("req").astype(jnp.int32).reshape(1)
    got1, me, *late = hold((got1, me, *late))
    part, gate, fresh, kept, c_main, b_main, decay, decay_t, step, step_t = late

    sent2, codes = pl.pallas_call(
        pack_second,
        out_shape=[packed((64, 48, 128), BF16), packed((8, 128), jnp.int32)],
        in_specs=[smem(), vmem(), pl.BlockSpec(memory_space=pl.ANY)],
        out_specs=[vmem(), smem()],
        scratch_shapes=[
            pltpu.VMEM((8, 128), jnp.int32), pltpu.VMEM((2, 64, 32, 128), BF16), pltpu.SemaphoreType.DMA((3,)),
        ],
        compiler_params=params(50),
        cost_estimate=cost(0, 3 << 20),
        name="pack_second",
    )(me, got1, states)
    got2 = exchange(sent2, "req")
    sent3 = pl.pallas_call(
        pack_third,
        out_shape=packed((64, 40, 128), BF16),
        in_specs=[smem(), vmem(), vmem()],
        out_specs=vmem(),
        compiler_params=params(52),
        cost_estimate=cost(0, 1 << 20),
        name="pack_third",
    )(codes, got1, got2)
    sent3, got2 = hold((sent3, got2))
    got3 = exchange(sent3, "req")
    held = lambda i: jnp.minimum(i, 7)
    part, fresh = pl.pallas_call(
        early_rows,
        out_shape=[packed((256, 2304), F32), packed((2048, 128), F32)],
        grid=(9,),
        in_specs=[
            pl.BlockSpec((16, 256), lambda i: (0, held(i))), whole(16, 2, 128),
            pl.BlockSpec((4, 256), lambda i: (0, held(i))), whole(4, 2, 128),
            pl.BlockSpec((64, 8, 128), lambda i: (0, 3, 0)),
            whole(1, 32), whole(256, 128), whole(256, 128), whole(32, 256), whole(256, 128), whole(32, 256),
            pl.BlockSpec((256, 256), lambda i: (0, held(i))), pl.BlockSpec((256, 128), lambda i: (held(i), 0)),
        ],
        out_specs=[cols(256, 256), pl.BlockSpec((256, 128), lambda i: (held(i), 0))],
        scratch_shapes=[
            pltpu.VMEM((16, 256), F32), pltpu.VMEM((16, 256), F32),
            pltpu.VMEM((256, 128), F32), pltpu.VMEM((128, 128), BF16), pltpu.VMEM((256, 128), BF16),
        ],
        compiler_params=params(52),
        cost_estimate=cost(1 << 29, 8 << 20),
        name="early_rows",
    )(
        inner_input, scan_args[1], inner_conv_taps, scan_args[3], got2, scan_args[7], c_main,
        decay, decay_t, step, step_t, part, fresh,
    )
    got3, part, fresh = hold((got3, part, fresh))

    normed, low = pl.pallas_call(
        state_kernel,
        out_shape=[packed((256, 2048), BF16), packed((8, 128, 128), BF16)],
        in_specs=[vmem(), far, far, vmem(), vmem()],
        out_specs=[far, far],
        scratch_shapes=[pltpu.VMEM((256, 2048), F32)] * 3
        + [pltpu.VMEM((128, 128), BF16), pltpu.VMEM((256, 128), F32), pltpu.VMEM((256, 2048), BF16), pltpu.SemaphoreType.DMA((2, 9))],
        compiler_params=params(52),
        cost_estimate=cost(1 << 28, 8 << 20),
        name="state",
    )(got3, part, gate, group_norm_gain.reshape(1, 2048), got2)
    low, fresh = hold((low, fresh))
    parts = exchange(low, "head")
    updated = pl.pallas_call(
        update_kernel,
        out_shape=packed((1, 2048, 128), BF16),
        in_specs=[vmem()] * 3,
        out_specs=vmem(),
        compiler_params=params(60),
        cost_estimate=cost(1 << 20, 3 << 20),
        name="update",
    )(got3, fresh, kept)
    parts, updated = hold((parts, updated))
    term = pl.pallas_call(
        up_kernel,
        out_shape=packed((256, 1024), BF16),
        in_specs=[vmem()] * 2,
        out_specs=vmem(),
        compiler_params=params(52),
        cost_estimate=cost(1 << 26, 1 << 20),
        name="up",
    )(parts, got3)
    return normed, term, updated.reshape(1, 32, 64, 128)


def solution(mesh):
    return jax.shard_map(
        per_device,
        mesh=mesh,
        in_specs=(
            P("req", "head"),
            P("req", "head", None, None),
            P("req", "head"),
            P(None, "head"),
            P(None, "head", None, None),
            P("head"),
            P("head"),
            P("head"),
            P("head"),
            P("req"),
            P(),
            P("req"),
            P("req"),
            P("req", "head", None),
            P("req", None, "head"),
            P("req", "head", None, None),
            P("req", None, "head"),
            P("req", None, "head", None, None),
        ),
        out_specs=(P("req", "head"), P("req", "head"), P("req", "head", None, None)),
        check_vma=False,
    )
```
